128 devices in a mesh: row: 8 (over z_lo, x), col: 16 (over z_hi, y, core).
Axes of the slice: x: 4, y: 4, z: 4 (z_hi: 2, z_lo: 2; z = z_hi * 2 + z_lo), core: 2. Of those that a mesh axis runs over, the one named last changes fastest.
Arguments:
- coarse_left: float32 [32, 16384], P('col', 'row'), may hold values from -3 to 3
- coarse_right: float32 [32, 16384], P('row', 'col'), may hold values from -3 to 3
- stencil_left: int32 [65536], P('row'), may hold values from -1 to 16384, as said below
- weights_left: float32 [4, 65536], P(None, 'row'), may hold values from 0.1 to 0.6
- stencil_right: int32 [65536], P('col'), may hold values from -1 to 16384, as said below
- weights_right: float32 [4, 65536], P(None, 'col'), may hold values from 0.1 to 0.6
- tile_mask: int32 [16, 16], P('row', 'col'), may hold values 0 or 1
- sample_rows: int32 [16, 16, 2048], P('row', 'col'), may hold values from 0 to 4095
- sample_cols: int32 [16, 16, 2048], P('row', 'col'), may hold values from 0 to 4095
- sample_values: float32 [16, 16, 2048], P('row', 'col'), may hold values from -6 to 6
Outputs:
- left_new: float32 [32, 65536], P('col', 'row')
- right_new: float32 [32, 65536], P('row', 'col')
The draws below stay inside these ranges and needn't reach their ends.
Inputs may be any that keep to these rules, and one draw needn't show every extreme that they name: stencil_left[i] is i // 4 - 1, i // 4 or i // 4 + 1. stencil_right[j] is j // 4 - 1, j // 4 or j // 4 + 1.
All inputs are finite; a program needn't handle non-finite values. No bound on the sum of `tile_mask` on one device may be relied on, other than what follows from the above.
Results may differ from the reference program's by a relative error of at most 0.0001.
Values sent between devices are 32-bit elements; how exact they have to be, the bound alone decides.
A program may use at most 64 MiB of HBM per device.

```python
import jax
import jax.numpy as jnp
from jax import lax

NF = 65536
NC = 16384
RANK = 32
TAPS = 4
TILES = 16
TILE = 4096
SPT = 2048


def draw_stencil_left(key, part):
    noise = jax.random.randint(jax.random.fold_in(key, 11), (NF,), -1, 2, dtype=jnp.int32)
    return (jnp.arange(NF, dtype=jnp.int32) // 4 + noise).astype(jnp.int32)


def draw_stencil_right(key, part):
    noise = jax.random.randint(jax.random.fold_in(key, 23), (NF,), -1, 2, dtype=jnp.int32)
    return (jnp.arange(NF, dtype=jnp.int32) // 4 + noise).astype(jnp.int32)


def with_ends(result, rng, smallest, top_value):
    longest = result.shape.index(max(result.shape))
    spots = []
    for shift in (0, 1):
        where = [jax.random.randint(jax.random.fold_in(rng, axis), (), 0, length) for axis, length in enumerate(result.shape)]
        where[longest] = (where[longest] + shift) % result.shape[longest]
        spots.append(tuple(where))
    return result.at[spots[0]].set(smallest).at[spots[1]].set(top_value)


def block_scale(key, shape, cuts, low, largest):
    def one(axis_at, parts):
        heights = jax.random.uniform(jax.random.fold_in(jax.random.fold_in(key, 6), axis_at), (parts,), jnp.float32, low / len(cuts), largest / len(cuts))
        return jnp.repeat(jnp.exp(heights), shape[axis_at] // parts).reshape((-1,) + (1,) * (len(shape) - axis_at - 1))

    gain = one(*cuts[0])
    for cut in cuts[1:]:
        gain = gain * one(*cut)
    return gain


def bell_draw(stream_key, shape, deviation, reach, shards=(), kind=jnp.bfloat16):
    factor_of = block_scale(stream_key, shape, shards, -0.22, 0.18) if shards else 1.0
    array = jax.random.normal(stream_key, shape, jnp.float32) * deviation * factor_of
    return jnp.minimum(jnp.maximum(array, -reach), reach).astype(kind)


def setup_inputs(seed: int = 0) -> dict:
    key_of = jax.random.split(jax.random.key(seed), 11)
    return {
        "coarse_left": bell_draw(key_of[0], (RANK, NC), 0.5, 3.0, ((0, 16), (1, 8)), jnp.float32),
        "coarse_right": bell_draw(key_of[1], (RANK, NC), 0.5, 3.0, ((0, 8), (1, 16)), jnp.float32),
        "stencil_left": draw_stencil_left(jax.random.fold_in(key_of[10], 71), 0),
        "weights_left": jnp.clip(0.1 + 0.5 * jax.random.uniform(key_of[3], (TAPS, NF), jnp.float32) ** block_scale(key_of[3], (TAPS, NF), ((1, 8),), -0.2, 0.2), 0.1, 0.6),
        "stencil_right": draw_stencil_right(jax.random.fold_in(key_of[10], 71), 0),
        "weights_right": jnp.clip(0.1 + 0.5 * jax.random.uniform(key_of[5], (TAPS, NF), jnp.float32) ** block_scale(key_of[5], (TAPS, NF), ((1, 16),), -0.2, 0.2), 0.1, 0.6),
        "tile_mask": with_ends((jax.random.randint(key_of[6], (TILES, TILES), 0, 2) < 1).astype(jnp.int32), jax.random.fold_in(key_of[6], 1), 0, 1),
        "sample_rows": with_ends(jax.random.randint(key_of[7], (TILES, TILES, SPT), 0, TILE), jax.random.fold_in(key_of[7], 1), 0, TILE - 1).astype(jnp.int32),
        "sample_cols": with_ends(jax.random.randint(key_of[8], (TILES, TILES, SPT), 0, TILE), jax.random.fold_in(key_of[8], 1), 0, TILE - 1).astype(jnp.int32),
        "sample_values": bell_draw(key_of[9], (TILES, TILES, SPT), 1.0, 6.0, ((0, 8), (1, 16)), jnp.float32),
    }


def spread(padded, base, weights, offset):
    start_at = base - offset + 2
    columns_at = start_at[None, :] + jnp.arange(4, dtype=jnp.int32)[:, None]
    values = jnp.take(padded, columns_at, axis=1)
    return jnp.sum(values * weights[None], axis=1)


def reference(coarse_left, coarse_right, stencil_left, weights_left, stencil_right, weights_right, tile_mask, sample_rows, sample_cols, sample_values):
    fine_left = spread(jnp.pad(coarse_left, ((0, 0), (3, 3))), stencil_left, weights_left, 0)
    fine_right = spread(jnp.pad(coarse_right, ((0, 0), (3, 3))), stencil_right, weights_right, 0)
    starts = jnp.arange(TILES, dtype=jnp.int32) * TILE
    row_start = jnp.broadcast_to(starts[:, None], (TILES, TILES)).reshape(-1)
    col_start = jnp.broadcast_to(starts[None, :], (TILES, TILES)).reshape(-1)
    rows_all = (sample_rows.reshape(TILES * TILES, SPT) + row_start[:, None]).astype(jnp.int32)
    cols_all = (sample_cols.reshape(TILES * TILES, SPT) + col_start[:, None]).astype(jnp.int32)
    values_all = sample_values.reshape(TILES * TILES, SPT)
    keeping = jnp.broadcast_to(tile_mask.reshape(-1, 1).astype(jnp.float32), (TILES * TILES, SPT))
    width = min(SPT, 4096)
    pieces = TILES * TILES * SPT // width
    rows_all = rows_all.reshape(pieces, width)
    cols_all = cols_all.reshape(pieces, width)
    values_all = values_all.reshape(pieces, width)
    keeping = keeping.reshape(pieces, width)

    def visit(carry, block):
        grad_left, grad_right = carry
        rows_here, cols_here, values_here, keep_here = block
        left_cols = jnp.take(fine_left, rows_here, axis=1)
        right_cols = jnp.take(fine_right, cols_here, axis=1)
        error = keep_here * (jnp.sum(left_cols * right_cols, axis=0) - values_here)
        grad_left = grad_left.at[:, rows_here].add(error[None, :] * right_cols)
        grad_right = grad_right.at[:, cols_here].add(error[None, :] * left_cols)
        return (grad_left, grad_right), None

    empty = jnp.zeros((RANK, NF), jnp.float32)
    (grad_left, grad_right), _ = lax.scan(visit, (empty, empty), (rows_all, cols_all, values_all, keeping))
    step_size = 4.0 * TILE / (SPT * TILES)
    return fine_left - step_size * grad_left, fine_right - step_size * grad_right
```

```python
import functools
import jax, jax.numpy as jnp
from jax import lax
from jax.sharding import PartitionSpec as P
from jax.experimental import pallas as pl
from jax.experimental.pallas import tpu as pltpu

TILE = 4096
SPT = 2048
LANES = 128
ETA = 0.5
f32, bf16, i32 = jnp.float32, jnp.bfloat16, jnp.int32


def lane_pick(table, index):
    return jnp.take_along_axis(table, index, axis=1)


def interpolate(coarse_ref, stencil_ref, weight_ref, fine_ref, origin, blocks):
    rank = coarse_ref.shape[0]
    groups = rank // 8

    @pl.loop(0, blocks)
    def _(b):
        at = pl.multiple_of(b * 128, 128)
        before = coarse_ref[:, pl.ds(at, 128)]
        here = coarse_ref[:, pl.ds(at + 128, 128)]
        after = coarse_ref[:, pl.ds(at + 256, 128)]
        low = jnp.concatenate([before[:, 64:], here[:, :64]], axis=1)
        high = jnp.concatenate([here[:, 64:], after[:, :64]], axis=1)
        for q, (window, shift) in enumerate(((low, 64), (here, 0), (here, 0), (high, -64))):
            fine_at = pl.multiple_of(b * 512 + q * 128, 128)
            base = stencil_ref[:, pl.ds(fine_at, 128)] - (origin + b * 128 - shift + 1)
            for g in range(groups):
                total = None
                for t in range(4):
                    index = jnp.broadcast_to(base + t, (8, 128))
                    picked = lane_pick(window[8 * g : 8 * g + 8], index)
                    term = picked * weight_ref[t : t + 1, pl.ds(fine_at, 128)]
                    total = term if total is None else total + term
                fine_ref[8 * g : 8 * g + 8, pl.ds(fine_at, 128)] = total


def pick_columns(fine_ref, start, position):
    hi = jnp.broadcast_to(position // 128, (8, 128))
    lo = jnp.broadcast_to(position % 128, (8, 128))
    got = [None] * 4
    for j in range(TILE // 128):
        mask = hi == j
        column = pl.multiple_of(start + j * 128, 128)
        for g in range(4):
            p = lane_pick(fine_ref[8 * g : 8 * g + 8, pl.ds(column, 128)], lo)
            got[g] = p if got[g] is None else jnp.where(mask, p, got[g])
    return got


def sublane_pick(x, first, period):
    index = first + lax.broadcasted_iota(i32, (8, 128), 0) % period
    return jnp.take_along_axis(x, index, axis=0)


def build_side(values, position, period, lhs_ref, ohot_ref, at, width):
    j = position // 128
    lane = position % 128
    half = 8 // period
    sel = (j // half) % 2
    hi = (j // (2 * half)) * half + j % half
    lo = sel * 128 + lane
    parts = 16 // (16 // period)
    row16 = lax.broadcasted_iota(i32, (16, 128), 0)
    tall = 16 // (16 // period)
    hi16 = jnp.broadcast_to(hi, (16, 128))
    per_tile = 16 // period
    masks = [
        jnp.where(hi16 == m * per_tile + row16 // period, 1.0, 0.0).astype(bf16)
        for m in range(16 // per_tile)
    ]
    slot_rows = 16 * len(masks)
    slot = 0
    for g in range(4):
        for first in range(0, 8, period):
            dup = sublane_pick(values[g], first, period)
            dup = jnp.concatenate([dup, dup], axis=0)
            top = dup.astype(bf16)
            rest = (dup - top.astype(f32)).astype(bf16)
            for m, mask in enumerate(masks):
                rows = slice(slot * slot_rows + 16 * m, slot * slot_rows + 16 * m + 16)
                lhs_ref[rows, pl.ds(at, 128)] = top * mask
                lhs_ref[rows, pl.ds(at + width, 128)] = rest * mask
            slot += 1
    lo256 = jnp.broadcast_to(lo, (256, 128))
    hot = jnp.where(lo256 == lax.broadcasted_iota(i32, (256, 128), 0), 1.0, 0.0).astype(bf16)
    ohot_ref[:, pl.ds(at, 128)] = hot
    ohot_ref[:, pl.ds(at + width, 128)] = hot


def add_side(lhs_ref, ohot_ref, out_ref, period, at):
    got = lax.dot_general(
        lhs_ref[...], ohot_ref[...], (((1,), (1,)), ((), ())), preferred_element_type=f32
    )
    slots = 32 // period
    groups = 64 // slots
    for slot in range(slots):
        for g in range(groups):
            for h in range(2):
                row = (slot * groups + g) * 8
                rows = pl.ds(pl.multiple_of(at + g * 16 + h * 8, 8), 8)
                out_ref[slot, rows, :] += got[row : row + 8, h * 128 : h * 128 + 128]


def add_own(fine_ref, out_ref, slot, period):
    group = pl.multiple_of((slot * period) // 8 * 8, 8)
    row = lax.broadcasted_iota(i32, (8, 128), 0)
    index = (slot * period) % 8 + row % period
    spread = 8 // period

    @pl.loop(0, 128 // 8)
    def _(block):
        got = None
        for q in range(spread):
            lanes = pl.ds(pl.multiple_of((block * spread + q) * 128, 128), 128)
            picked = jnp.take_along_axis(fine_ref[pl.ds(group, 8), lanes], index, axis=0)
            got = picked if got is None else jnp.where(row // period == q, picked, got)
        out_ref[slot, pl.ds(pl.multiple_of(block * 8, 8), 8), :] += got


CHUNK = 512


def local_kernel(
    mask_ref, left_ref, right_ref, sl_ref, wl_ref, sr_ref, wr_ref, rows_ref, cols_ref, vals_ref,
    ol_ref, or_ref, fl_ref, fr_ref, lhs_ref, ohot_ref,
):
    my_row = lax.axis_index("row")
    my_col = lax.axis_index("col")
    interpolate(left_ref, sl_ref, wl_ref, fl_ref, my_row * 2048, 16)
    interpolate(right_ref, sr_ref, wr_ref, fr_ref, my_col * 1024, 8)
    ol_ref[...] = jnp.zeros(ol_ref.shape, f32)
    or_ref[...] = jnp.zeros(or_ref.shape, f32)

    per_tile = SPT // CHUNK

    @pl.loop(0, 2 * per_tile)
    def _(step):
        tile = step // per_tile
        first = (step % per_tile) * CHUNK
        keep = mask_ref[tile, 0].astype(f32) * -ETA

        @pl.loop(0, CHUNK // 128)
        def _(sub):
            at = pl.multiple_of(sub * 128, 128)
            s_at = pl.multiple_of(first + sub * 128, 128)
            row = rows_ref[tile, :, pl.ds(s_at, 128)]
            col = cols_ref[tile, :, pl.ds(s_at, 128)]
            left = pick_columns(fl_ref, tile * TILE, row)
            right = pick_columns(fr_ref, 0, col)
            dots = sum(left[g] * right[g] for g in range(4))
            error = jnp.sum(dots, axis=0, keepdims=True) - vals_ref[tile, :, pl.ds(s_at, 128)]
            scaled = error * keep
            build_side([scaled * right[g] for g in range(4)], row, 2, lhs_ref.at[0], ohot_ref.at[0], at, CHUNK)
            build_side([scaled * left[g] for g in range(4)], col, 4, lhs_ref.at[1], ohot_ref.at[1], at, CHUNK)

        add_side(lhs_ref.at[0], ohot_ref.at[0], ol_ref, 2, tile * 64)
        add_side(lhs_ref.at[1], ohot_ref.at[1], or_ref, 4, 0)

    add_own(fl_ref, ol_ref, my_col, 2)
    add_own(fr_ref, or_ref, my_row, 4)


def local_step(mask, left, right, sl, wl, sr, wr, rows, cols, vals):
    vmem = pl.BlockSpec(memory_space=pltpu.VMEM)
    return pl.pallas_call(
        local_kernel,
        out_shape=(
            jax.ShapeDtypeStruct((16, 128, 128), f32),
            jax.ShapeDtypeStruct((8, 128, 128), f32),
        ),
        in_specs=[pl.BlockSpec(memory_space=pltpu.SMEM)] + [vmem] * 9,
        out_specs=(vmem, vmem),
        scratch_shapes=[
            pltpu.VMEM((32, 8192), f32),
            pltpu.VMEM((32, 4096), f32),
            pltpu.VMEM((2, 512, 2 * CHUNK), bf16),
            pltpu.VMEM((2, 256, 2 * CHUNK), bf16),
        ],
        name="local_step",
    )(mask, left, right, sl.reshape(1, -1), wl, sr.reshape(1, -1), wr, rows, cols, vals)


def with_halo(block, axis):
    count = lax.axis_size(axis)
    forward = [(i, i + 1) for i in range(count - 1)]
    backward = [(i + 1, i) for i in range(count - 1)]
    low = lax.ppermute(block[:, -128:], axis, forward)
    high = lax.ppermute(block[:, :128], axis, backward)
    return jnp.concatenate([low, block, high], axis=1)


def sum_at_owner(parts, axis):
    return jnp.sum(lax.all_to_all(parts, axis, 0, 0, tiled=True), axis=0)


def on_device(coarse_left, coarse_right, sl, wl, sr, wr, mask, rows, cols, vals):
    left = lax.all_gather(with_halo(coarse_left, "row"), "col", axis=0, tiled=True)
    right = lax.all_gather(with_halo(coarse_right, "col"), "row", axis=0, tiled=True)
    gl, gr = local_step(mask, left, right, sl, wl, sr, wr, rows, cols, vals)
    left_new = sum_at_owner(gl, "col").reshape(64, 2, 128).transpose(1, 0, 2).reshape(2, 8192)
    right_new = sum_at_owner(gr, "row").reshape(32, 4, 128).transpose(1, 0, 2).reshape(4, 4096)
    return left_new, right_new


def solution(mesh):
    in_specs = (
        P("col", "row"),
        P("row", "col"),
        P("row"),
        P(None, "row"),
        P("col"),
        P(None, "col"),
        P("row", "col"),
        P("row", "col", None),
        P("row", "col", None),
        P("row", "col", None),
    )
    out_specs = (P("col", "row"), P("row", "col"))
    return jax.shard_map(
        on_device, mesh=mesh, in_specs=in_specs, out_specs=out_specs, check_vma=False
    )
```

```python
import functools
import jax, jax.numpy as jnp
from jax import lax
from jax.sharding import PartitionSpec as P
from jax.experimental import pallas as pl
from jax.experimental.pallas import tpu as pltpu

TILE = 4096
SPT = 2048
LANES = 128
ETA = 0.5
f32, bf16, i32 = jnp.float32, jnp.bfloat16, jnp.int32


def lane_pick(table, index):
    return jnp.take_along_axis(table, index, axis=1)


def interpolate(coarse_ref, stencil_ref, weight_ref, fine_ref, origin, blocks):
    rank = coarse_ref.shape[0]
    groups = rank // 8

    @pl.loop(0, blocks)
    def _(b):
        at = pl.multiple_of(b * 128, 128)
        ahead = pl.multiple_of((b + blocks + 1) % (blocks + 2) * 128, 128)
        before = coarse_ref[:, pl.ds(ahead, 128)]
        here = coarse_ref[:, pl.ds(at, 128)]
        after = coarse_ref[:, pl.ds(pl.multiple_of(at + 128, 128), 128)]
        low = jnp.concatenate([before[:, 64:], here[:, :64]], axis=1)
        high = jnp.concatenate([here[:, 64:], after[:, :64]], axis=1)
        for q, (window, shift) in enumerate(((low, 64), (here, 0), (here, 0), (high, -64))):
            fine_at = pl.multiple_of(b * 512 + q * 128, 128)
            base = stencil_ref[:, pl.ds(fine_at, 128)] - (origin + b * 128 - shift + 1)
            for g in range(groups):
                total = None
                for t in range(4):
                    index = jnp.broadcast_to(base + t, (8, 128))
                    picked = lane_pick(window[8 * g : 8 * g + 8], index)
                    term = picked * weight_ref[t : t + 1, pl.ds(fine_at, 128)]
                    total = term if total is None else total + term
                fine_ref[8 * g : 8 * g + 8, pl.ds(fine_at, 128)] = total


def pick_columns(fine_ref, start, position):
    hi = jnp.broadcast_to(position // 128, (8, 128))
    lo = jnp.broadcast_to(position % 128, (8, 128))
    got = [None] * 4
    for j in range(TILE // 128):
        mask = hi == j
        column = pl.multiple_of(start + j * 128, 128)
        for g in range(4):
            p = lane_pick(fine_ref[8 * g : 8 * g + 8, pl.ds(column, 128)], lo)
            got[g] = p if got[g] is None else jnp.where(mask, p, got[g])
    return got


def sublane_pick(x, first, period):
    index = first + lax.broadcasted_iota(i32, (8, 128), 0) % period
    return jnp.take_along_axis(x, index, axis=0)


def build_side(values, position, period, lhs_ref, ohot_ref, at, width):
    j = position // 128
    lane = position % 128
    half = 8 // period
    sel = (j // half) % 2
    hi = (j // (2 * half)) * half + j % half
    lo = sel * 128 + lane
    parts = 16 // (16 // period)
    row16 = lax.broadcasted_iota(i32, (16, 128), 0)
    tall = 16 // (16 // period)
    hi16 = jnp.broadcast_to(hi, (16, 128))
    per_tile = 16 // period
    masks = [
        jnp.where(hi16 == m * per_tile + row16 // period, 1.0, 0.0).astype(bf16)
        for m in range(16 // per_tile)
    ]
    slot_rows = 16 * len(masks)
    slot = 0
    for g in range(4):
        for first in range(0, 8, period):
            dup = sublane_pick(values[g], first, period)
            dup = jnp.concatenate([dup, dup], axis=0)
            top = dup.astype(bf16)
            rest = (dup - top.astype(f32)).astype(bf16)
            for m, mask in enumerate(masks):
                rows = slice(slot * slot_rows + 16 * m, slot * slot_rows + 16 * m + 16)
                lhs_ref[rows, pl.ds(at, 128)] = top * mask
                lhs_ref[rows, pl.ds(at + width, 128)] = rest * mask
            slot += 1
    lo256 = jnp.broadcast_to(lo, (256, 128))
    hot = jnp.where(lo256 == lax.broadcasted_iota(i32, (256, 128), 0), 1.0, 0.0).astype(bf16)
    ohot_ref[:, pl.ds(at, 128)] = hot
    ohot_ref[:, pl.ds(at + width, 128)] = hot


def left_place(slot):
    return slot % 2 * 8 + slot // 2 % 4 * 2 + slot // 8


def right_place(slot):
    return slot % 4 * 2 + slot // 4


def add_side(lhs_ref, ohot_ref, out_ref, period, place, at):
    got = lax.dot_general(
        lhs_ref[...], ohot_ref[...], (((1,), (1,)), ((), ())), preferred_element_type=f32
    )
    slots = 32 // period
    groups = 64 // slots
    for slot in range(slots):
        for g in range(groups):
            for h in range(2):
                row = (slot * groups + g) * 8
                rows = pl.ds(pl.multiple_of(at + g * 16 + h * 8, 8), 8)
                out_ref[place(slot), rows, :] += got[row : row + 8, h * 128 : h * 128 + 128]


def add_own(fine_ref, out_ref, slot, period, place):
    group = pl.multiple_of((slot * period) // 8 * 8, 8)
    row = lax.broadcasted_iota(i32, (8, 128), 0)
    index = (slot * period) % 8 + row % period
    spread = 8 // period

    @pl.loop(0, 128 // 8)
    def _(block):
        got = None
        for q in range(spread):
            lanes = pl.ds(pl.multiple_of((block * spread + q) * 128, 128), 128)
            picked = jnp.take_along_axis(fine_ref[pl.ds(group, 8), lanes], index, axis=0)
            got = picked if got is None else jnp.where(row // period == q, picked, got)
        out_ref[place(slot), pl.ds(pl.multiple_of(block * 8, 8), 8), :] += got


CHUNK = 512


def local_kernel(
    mask_ref, left_ref, right_ref, sl_ref, wl_ref, sr_ref, wr_ref, rows_ref, cols_ref, vals_ref,
    ol_ref, or_ref, fl_ref, fr_ref, lhs_ref, ohot_ref,
):
    my_row = lax.axis_index("row")
    my_col = lax.axis_index("col")
    interpolate(left_ref, sl_ref, wl_ref, fl_ref, my_row * 2048, 16)
    interpolate(right_ref, sr_ref, wr_ref, fr_ref, my_col * 1024, 8)
    ol_ref[...] = jnp.zeros(ol_ref.shape, f32)
    or_ref[...] = jnp.zeros(or_ref.shape, f32)

    per_tile = SPT // CHUNK

    @pl.loop(0, 2 * per_tile)
    def _(step):
        tile = step // per_tile
        first = (step % per_tile) * CHUNK
        keep = mask_ref[tile, 0].astype(f32) * -ETA

        @pl.loop(0, CHUNK // 128)
        def _(sub):
            at = pl.multiple_of(sub * 128, 128)
            s_at = pl.multiple_of(first + sub * 128, 128)
            row = rows_ref[tile, :, pl.ds(s_at, 128)]
            col = cols_ref[tile, :, pl.ds(s_at, 128)]
            left = pick_columns(fl_ref, tile * TILE, row)
            right = pick_columns(fr_ref, 0, col)
            dots = sum(left[g] * right[g] for g in range(4))
            error = jnp.sum(dots, axis=0, keepdims=True) - vals_ref[tile, :, pl.ds(s_at, 128)]
            scaled = error * keep
            build_side([scaled * right[g] for g in range(4)], row, 2, lhs_ref.at[0], ohot_ref.at[0], at, CHUNK)
            build_side([scaled * left[g] for g in range(4)], col, 4, lhs_ref.at[1], ohot_ref.at[1], at, CHUNK)

        add_side(lhs_ref.at[0], ohot_ref.at[0], ol_ref, 2, left_place, tile * 64)
        add_side(lhs_ref.at[1], ohot_ref.at[1], or_ref, 4, right_place, 0)

    add_own(fl_ref, ol_ref, my_col, 2, left_place)
    add_own(fr_ref, or_ref, my_row, 4, right_place)


def local_step(mask, left, right, sl, wl, sr, wr, rows, cols, vals):
    vmem = pl.BlockSpec(memory_space=pltpu.VMEM)
    return pl.pallas_call(
        local_kernel,
        out_shape=(
            jax.ShapeDtypeStruct((16, 128, 128), f32),
            jax.ShapeDtypeStruct((8, 128, 128), f32),
        ),
        in_specs=[pl.BlockSpec(memory_space=pltpu.SMEM)] + [vmem] * 9,
        out_specs=(vmem, vmem),
        scratch_shapes=[
            pltpu.VMEM((32, 8192), f32),
            pltpu.VMEM((32, 4096), f32),
            pltpu.VMEM((2, 512, 2 * CHUNK), bf16),
            pltpu.VMEM((2, 256, 2 * CHUNK), bf16),
        ],
        name="local_step",
    )(mask, left, right, sl.reshape(1, -1), wl, sr.reshape(1, -1), wr, rows, cols, vals)


MESH_ID = pl.DeviceIdType.MESH


def greet(others):
    barrier = pltpu.get_barrier_semaphore()
    for other in others:
        pl.semaphore_signal(barrier, inc=1, device_id=other, device_id_type=MESH_ID)
    pl.semaphore_wait(barrier, len(others))


def gather_kernel(
    cl_ref, cr_ref, gl_ref, gr_ref, edge_send, edge_recv, main_send, main_recv, halo_send, halo_recv
):
    r = lax.axis_index("row")
    c = lax.axis_index("col")
    col_peers = [(r, (c + d) % 16) for d in range(1, 16)]
    row_peers = [((r + d) % 8, c) for d in range(1, 8)]
    greet(col_peers + row_peers)

    def send(src, dst, sems, at, to):
        copy = pltpu.make_async_remote_copy(
            src_ref=src, dst_ref=dst, send_sem=sems[0].at[at], recv_sem=sems[1].at[at],
            device_id=to, device_id_type=MESH_ID,
        )
        copy.start()
        return copy

    edges = (edge_send, edge_recv)
    mains = (main_send, main_recv)
    halos = (halo_send, halo_recv)
    edge_copies = [
        send(cl_ref.at[:, 0:128], gl_ref.at[c, :, 2048:2176], edges, 0, ((r + 7) % 8, c)),
        send(cl_ref.at[:, 1920:2048], gl_ref.at[c, :, 2176:2304], edges, 1, ((r + 1) % 8, c)),
        send(cr_ref.at[:, 0:128], gr_ref.at[r, :, 1024:1152], edges, 2, (r, (c + 15) % 16)),
        send(cr_ref.at[:, 896:1024], gr_ref.at[r, :, 1152:1280], edges, 3, (r, (c + 1) % 16)),
    ]
    main_copies = [
        send(cl_ref, gl_ref.at[c, :, 0:2048], mains, d, (r, (c + d) % 16)) for d in range(1, 16)
    ] + [
        send(cr_ref, gr_ref.at[r, :, 0:1024], mains, 15 + d, ((r + d) % 8, c)) for d in range(1, 8)
    ]
    gl_ref[c, :, 0:2048] = cl_ref[...]
    gr_ref[r, :, 0:1024] = cr_ref[...]
    for copy in edge_copies:
        copy.wait()
    halo_copies = [
        send(gl_ref.at[c, :, 2048:2304], gl_ref.at[c, :, 2048:2304], halos, d, (r, (c + d) % 16))
        for d in range(1, 16)
    ] + [
        send(gr_ref.at[r, :, 1024:1280], gr_ref.at[r, :, 1024:1280], halos, 15 + d, ((r + d) % 8, c))
        for d in range(1, 8)
    ]
    for copy in main_copies:
        copy.wait()
    for copy in halo_copies:
        copy.wait()

    @pl.when(r == 0)
    def _():
        gl_ref[:, :, 2176:2304] = jnp.zeros((16, 2, 128), f32)

    @pl.when(r == 7)
    def _():
        gl_ref[:, :, 2048:2176] = jnp.zeros((16, 2, 128), f32)

    @pl.when(c == 0)
    def _():
        gr_ref[:, :, 1152:1280] = jnp.zeros((8, 4, 128), f32)

    @pl.when(c == 15)
    def _():
        gr_ref[:, :, 1024:1152] = jnp.zeros((8, 4, 128), f32)


def gather_coarse(coarse_left, coarse_right):
    vmem = pl.BlockSpec(memory_space=pltpu.VMEM)
    dma = pltpu.SemaphoreType.DMA
    return pl.pallas_call(
        gather_kernel,
        out_shape=(
            jax.ShapeDtypeStruct((16, 2, 2304), f32),
            jax.ShapeDtypeStruct((8, 4, 1280), f32),
        ),
        in_specs=[vmem, vmem],
        out_specs=(vmem, vmem),
        scratch_shapes=[dma((4,)), dma((4,)), dma((23,)), dma((23,)), dma((23,)), dma((23,))],
        compiler_params=pltpu.CompilerParams(collective_id=0, has_side_effects=True),
        name="gather_coarse",
    )(coarse_left, coarse_right)


PIECES = 2


def reduce_kernel(
    gl_ref, gr_ref, ol_ref, or_ref,
    pair_ref, sum_ref, ly_ref, lsum_ref, lz_ref, rx_ref, rsum_ref, rz_ref, sends, recvs,
):
    r = lax.axis_index("row")
    c = lax.axis_index("col")
    zlo, x = r // 4, r % 4
    zhi, y, core = c // 8, (c // 2) % 4, c % 2
    pair = (r, c + 1 - 2 * core)
    y_peer = [(r, zhi * 8 + ((y + d) % 4) * 2 + core) for d in range(1, 4)]
    x_peer = [(zlo * 4 + (x + d) % 4, c) for d in range(1, 4)]
    left_z = (r, (c + 8) % 16)
    right_z = ((r + 4) % 8, c)
    greet([pair, left_z, right_z] + y_peer + x_peer)
    rows = 128 // PIECES

    def send(src, dst, at, to):
        copy = pltpu.make_async_remote_copy(
            src_ref=src, dst_ref=dst, send_sem=sends.at[at], recv_sem=recvs.at[at],
            device_id=to, device_id_type=MESH_ID,
        )
        copy.start()
        return copy

    started = []
    cut = [pl.ds(p * rows, rows) for p in range(PIECES)]
    to_pair = [
        send(gl_ref.at[pl.ds((1 - core) * 8, 8), cut[p]], pair_ref.at[:, cut[p]], p * 9, pair)
        for p in range(PIECES)
    ]
    to_x = [
        [
            send(
                gr_ref.at[pl.ds(((x + d) % 4) * 2, 2), cut[p]], rx_ref.at[d - 1, :, cut[p]],
                p * 9 + d, x_peer[d - 1],
            )
            for d in range(1, 4)
        ]
        for p in range(PIECES)
    ]
    to_y = []
    for p in range(PIECES):
        to_pair[p].wait()
        for s in range(8):
            sum_ref[s, cut[p]] = gl_ref[core * 8 + s, cut[p]] + pair_ref[s, cut[p]]
        to_y.append([
            send(
                sum_ref.at[pl.ds(((y + d) % 4) * 2, 2), cut[p]], ly_ref.at[d - 1, :, cut[p]],
                p * 9 + 3 + d, y_peer[d - 1],
            )
            for d in range(1, 4)
        ])
    to_rz, to_lz = [], []
    for p in range(PIECES):
        for copy in to_x[p]:
            copy.wait()
        for s in range(2):
            rsum_ref[s, cut[p]] = gr_ref[x * 2 + s, cut[p]] + (
                rx_ref[0, s, cut[p]] + rx_ref[1, s, cut[p]] + rx_ref[2, s, cut[p]]
            )
        to_rz.append(send(rsum_ref.at[1 - zlo, cut[p]], rz_ref.at[cut[p]], p * 9 + 7, right_z))
        for copy in to_y[p]:
            copy.wait()
        for s in range(2):
            lsum_ref[s, cut[p]] = sum_ref[y * 2 + s, cut[p]] + (
                ly_ref[0, s, cut[p]] + ly_ref[1, s, cut[p]] + ly_ref[2, s, cut[p]]
            )
        to_lz.append(send(lsum_ref.at[1 - zhi, cut[p]], lz_ref.at[cut[p]], p * 9 + 8, left_z))
    for p in range(PIECES):
        to_rz[p].wait()
        or_ref[cut[p]] = rsum_ref[zlo, cut[p]] + rz_ref[cut[p]]
        to_lz[p].wait()
        ol_ref[cut[p]] = lsum_ref[zhi, cut[p]] + lz_ref[cut[p]]


def reduce_grads(gl, gr):
    vmem = pl.BlockSpec(memory_space=pltpu.VMEM)
    dma = pltpu.SemaphoreType.DMA
    block = (128, 128)
    return pl.pallas_call(
        reduce_kernel,
        out_shape=(jax.ShapeDtypeStruct(block, f32), jax.ShapeDtypeStruct(block, f32)),
        in_specs=[vmem, vmem],
        out_specs=(vmem, vmem),
        scratch_shapes=[
            pltpu.VMEM((8, *block), f32),
            pltpu.VMEM((8, *block), f32),
            pltpu.VMEM((3, 2, *block), f32),
            pltpu.VMEM((2, *block), f32),
            pltpu.VMEM(block, f32),
            pltpu.VMEM((3, 2, *block), f32),
            pltpu.VMEM((2, *block), f32),
            pltpu.VMEM(block, f32),
            dma((9 * PIECES,)),
            dma((9 * PIECES,)),
        ],
        compiler_params=pltpu.CompilerParams(collective_id=1, has_side_effects=True),
        name="reduce_grads",
    )(gl, gr)


def on_device(coarse_left, coarse_right, sl, wl, sr, wr, mask, rows, cols, vals):
    left, right = gather_coarse(coarse_left, coarse_right)
    gl, gr = local_step(mask, left.reshape(32, 2304), right.reshape(32, 1280), sl, wl, sr, wr, rows, cols, vals)
    left_sum, right_sum = reduce_grads(gl, gr)
    left_new = left_sum.reshape(64, 2, 128).transpose(1, 0, 2).reshape(2, 8192)
    right_new = right_sum.reshape(32, 4, 128).transpose(1, 0, 2).reshape(4, 4096)
    return left_new, right_new


def solution(mesh):
    in_specs = (
        P("col", "row"),
        P("row", "col"),
        P("row"),
        P(None, "row"),
        P("col"),
        P(None, "col"),
        P("row", "col"),
        P("row", "col", None),
        P("row", "col", None),
        P("row", "col", None),
    )
    out_specs = (P("col", "row"), P("row", "col"))
    return jax.shard_map(
        on_device, mesh=mesh, in_specs=in_specs, out_specs=out_specs, check_vma=False
    )
```

```python
import functools
import jax, jax.numpy as jnp
from jax import lax
from jax.sharding import PartitionSpec as P
from jax.experimental import pallas as pl
from jax.experimental.pallas import tpu as pltpu

TILE = 4096
SPT = 2048
BLOCK = 512
BLOCKS = 2 * SPT // BLOCK
PER_TILE = SPT // BLOCK
ETA = 0.5
f32, bf16, i32 = jnp.float32, jnp.bfloat16, jnp.int32


def lanes(at, size=128):
    return pl.ds(pl.multiple_of(at, 128), size)


def lane_pick(table, index):
    return jnp.take_along_axis(table, index, axis=1)


LEFT_STEPS, RIGHT_STEPS = 17, 9
PAD = 384


def upsample_matrix(up_ref):
    row = lax.broadcasted_iota(i32, (16, 128), 0)
    lane = lax.broadcasted_iota(i32, (16, 128), 1)
    for pattern in range(2):
        for offset in range(6):
            gap = (32 * pattern + 30 + offset + (lane >> 2) - row).astype(f32).astype(bf16)
            one, zero = jnp.ones((16, 128), bf16), jnp.zeros((16, 128), bf16)
            for m in range(8):
                part = jnp.where(gap == jnp.full((16, 128), 16 * m, bf16), one, zero)
                at = (pattern * 6 + offset) * 128
                up_ref[16 * m : 16 * m + 16, at : at + 128] = part
                up_ref[128 + 16 * m : 144 + 16 * m, at : at + 128] = part


def spread_weights(stencil_ref, weight_ref, by_offset_ref, origin, count):
    row = lax.broadcasted_iota(i32, (8, 128), 0)
    lane = lax.broadcasted_iota(i32, (8, 128), 1)

    def step(block, _):
        weight = jnp.concatenate(
            [weight_ref[:, lanes(block * 128)], jnp.zeros((4, 128), f32)], axis=0
        )
        stencil = jnp.broadcast_to(stencil_ref[:, lanes(block * 128)], (8, 128))
        base = stencil - (origin + block * 32) - (lane >> 2)
        by_offset_ref[:, lanes(block * 128 + PAD)] = jnp.take_along_axis(
            weight, (row - 1 - base) & 7, axis=0
        )
        return 0

    lax.fori_loop(0, count // 128, step, 0, unroll=4)


def two_terms(value):
    top = value.astype(bf16)
    return top, (value - top.astype(f32)).astype(bf16)


def coarse_windows(coarse, lhs_ref, base, steps):
    def step(b, _):
        here = coarse((b + steps) % (steps + 1))
        after = coarse(b)
        mid = jnp.concatenate([here[:, 64:], after[:, :64]], axis=1)
        for w, window in enumerate((here, mid)):
            top, rest = two_terms(window)
            rows = pl.ds(pl.multiple_of(base + b * 64 + w * 32, 32), 32)
            lhs_ref[rows, 0:128] = top
            lhs_ref[rows, 128:256] = rest
        return 0

    lax.fori_loop(0, steps, step, 0)


def interpolate(lhs_ref, up_ref, by_offset_ref, fine_ref, base, steps):
    for tile in range(6):
        pattern, first = tile // 3, tile % 3 * 2
        got = jnp.dot(
            lhs_ref[base : base + steps * 64, :],
            up_ref[:, tile * 256 : tile * 256 + 256],
            preferred_element_type=f32,
        )
        for b in range(steps):
            for w in range(2):
                at = slice(b * 512 + (2 * w + pattern) * 128, b * 512 + (2 * w + pattern) * 128 + 128)
                weight = [
                    jnp.broadcast_to(by_offset_ref[first + n : first + n + 1, at], (8, 128))
                    for n in range(2)
                ]
                for g in range(4):
                    row = b * 64 + w * 32 + g * 8
                    part = got[row : row + 8, 0:128] * weight[0] + got[row : row + 8, 128:256] * weight[1]
                    if first:
                        part = part + fine_ref[8 * g : 8 * g + 8, at]
                    fine_ref[8 * g : 8 * g + 8, at] = part


def pick_columns(fine_ref, start, position):
    j = jnp.broadcast_to(position >> 7, (8, 128))
    lo = jnp.broadcast_to(position & 127, (8, 128))
    bits = [(j & (1 << b)) != 0 for b in range(5)]

    def tree(g, prefix, bit):
        if bit < 0:
            return lane_pick(fine_ref[8 * g : 8 * g + 8, lanes(PAD + start + prefix * 128)], lo)
        off = tree(g, prefix, bit - 1)
        on = tree(g, prefix | 1 << bit, bit - 1)
        return jnp.where(bits[bit], on, off)

    return [tree(g, 0, 4) for g in range(4)]


def build_table(fine_ref, table_ref):
    def step(hi, _):
        for h in range(2):
            j = (hi >> 1) * 4 + h * 2 + (hi & 1)
            for half in range(2):
                v = fine_ref[16 * half : 16 * half + 16, lanes(PAD + j * 128)]
                top, rest = two_terms(v)
                rows = pl.ds(pl.multiple_of(hi * 32 + 16 * half, 16), 16)
                table_ref[rows, h * 128 : h * 128 + 128] = top
                table_ref[rows, 256 + h * 128 : 384 + h * 128] = rest
        return 0

    lax.fori_loop(0, 16, step, 0, unroll=4)


def one_hot(lo):
    lo16 = jnp.broadcast_to(lo, (16, 128)) - lax.broadcasted_iota(i32, (16, 128), 0)
    lo16 = lo16.astype(f32).astype(bf16)
    one, zero = jnp.ones((16, 128), bf16), jnp.zeros((16, 128), bf16)
    return jnp.concatenate(
        [jnp.where(lo16 == jnp.full((16, 128), 16 * m, bf16), one, zero) for m in range(16)], axis=0
    )


def table_columns(table_ref, positions):
    split = [split_position(p, 4) for p in positions]
    hot = jnp.concatenate([one_hot(lo) for _, lo in split], axis=1)
    rhs = jnp.concatenate([hot, hot], axis=0)
    got = jnp.dot(table_ref[...], rhs, preferred_element_type=f32)
    out = []
    for sub, (hi, _) in enumerate(split):
        hi8 = jnp.broadcast_to(hi, (8, 128))
        bits = [(hi8 & (1 << b)) != 0 for b in range(4)]

        def tree(g, prefix, bit):
            if bit < 0:
                row = prefix * 32 + 8 * g
                return got[row : row + 8, sub * 128 : sub * 128 + 128]
            return jnp.where(bits[bit], tree(g, prefix | 1 << bit, bit - 1), tree(g, prefix, bit - 1))

        out.append([tree(g, 0, 3) for g in range(4)])
    return out


def sample_block(blk, fl_ref, table_ref, vl_ref, vr_ref, rows_ref, cols_ref, vals_ref, mask_ref):
    tile = blk // PER_TILE
    subs = [(blk % PER_TILE) * BLOCK + sub * 128 for sub in range(BLOCK // 128)]
    rights = table_columns(table_ref, [cols_ref[tile, :, lanes(at)] for at in subs])
    keep = mask_ref[0, tile].astype(f32) * -ETA
    for sub, at in enumerate(subs):
        left = pick_columns(fl_ref, tile * TILE, rows_ref[tile, :, lanes(at)])
        right = rights[sub]
        dots = (left[0] * right[0] + left[1] * right[1]) + (left[2] * right[2] + left[3] * right[3])
        error = jnp.sum(dots, axis=0, keepdims=True) - vals_ref[tile, :, lanes(at)]
        scaled = jnp.broadcast_to(error * keep, (8, 128))
        out = lanes(blk * BLOCK + sub * 128)
        for g in range(4):
            vl_ref[8 * g : 8 * g + 8, out] = scaled * right[g]
            vr_ref[8 * g : 8 * g + 8, out] = scaled * left[g]


def split_position(position, period):
    half = 8 // period
    j = position >> 7
    hi = (j // (2 * half)) * half + (j & (half - 1))
    lo = ((j // half) & 1) * 128 + (position & 127)
    return hi, lo


def scatter_block(blk, value_ref, position_ref, out_ref, period, place, at):
    tile = blk // PER_TILE
    per_tile = 16 // period
    count = 16 // per_tile
    row16 = lax.broadcasted_iota(i32, (16, 128), 0)
    hots, tops, rests = [], [], []
    for sub in range(BLOCK // 128):
        position = position_ref[tile, :, lanes((blk % PER_TILE) * BLOCK + sub * 128)]
        hi, lo = split_position(position, period)
        hi16 = jnp.broadcast_to(hi, (16, 128)) - row16 // period
        masks = [jnp.where(hi16 == m * per_tile, 1.0, 0.0).astype(bf16) for m in range(count)]
        hots.append(one_hot(lo))
        top_rows, rest_rows = [], []
        for g in range(4):
            v = value_ref[8 * g : 8 * g + 8, lanes(blk * BLOCK + sub * 128)]
            for first in range(0, 8, period):
                index = first + lax.broadcasted_iota(i32, (8, 128), 0) % period
                dup = jnp.take_along_axis(v, index, axis=0)
                dup = jnp.concatenate([dup, dup], axis=0)
                top, rest = two_terms(dup)
                for mask in masks:
                    top_rows.append(top * mask)
                    rest_rows.append(rest * mask)
        tops.append(top_rows)
        rests.append(rest_rows)
    pieces = [jnp.concatenate(p, axis=0) for p in tops + rests]
    lhs = jnp.concatenate(pieces, axis=1)
    rhs = jnp.concatenate(hots + hots, axis=1)
    got = lax.dot_general(lhs, rhs, (((1,), (1,)), ((), ())), preferred_element_type=f32)
    slots = 32 // period
    groups = 64 // slots
    for slot in range(slots):
        for g in range(groups):
            for h in range(2):
                row = (slot * groups + g) * 8
                rows = pl.ds(pl.multiple_of(at + g * 16 + h * 8, 8), 8)
                out_ref[place(slot), rows, :] += got[row : row + 8, h * 128 : h * 128 + 128]


def left_place(slot):
    return slot % 2 * 8 + slot // 2 % 4 * 2 + slot // 8


def right_place(slot):
    return slot % 4 * 2 + slot // 4


def add_own(fine_ref, out_ref, slot, period, place):
    group = pl.multiple_of((slot * period) // 8 * 8, 8)
    row = lax.broadcasted_iota(i32, (8, 128), 0)
    index = (slot * period) % 8 + row % period
    spread = 8 // period

    def step(block, _):
        got = None
        for q in range(spread):
            tall = fine_ref[pl.ds(group, 8), lanes(PAD + (block * spread + q) * 128)]
            picked = jnp.take_along_axis(tall, index, axis=0)
            got = picked if got is None else jnp.where(row // period == q, picked, got)
        out_ref[place(slot), pl.ds(pl.multiple_of(block * 8, 8), 8), :] = got
        return 0

    lax.fori_loop(0, 16, step, 0, unroll=4)


MESH_ID = pl.DeviceIdType.MESH


def greet(others):
    barrier = pltpu.get_barrier_semaphore()
    for other in others:
        pl.semaphore_signal(barrier, inc=1, device_id=other, device_id_type=MESH_ID)
    pl.semaphore_wait(barrier, len(others))


def gather_coarse(
    r, c, cl_ref, cr_ref, gl_ref, gr_ref, edge_send, edge_recv, main_send, main_recv, halo_send, halo_recv
):
    def send(src, dst, sems, at, to):
        copy = pltpu.make_async_remote_copy(
            src_ref=src, dst_ref=dst, send_sem=sems[0].at[at], recv_sem=sems[1].at[at],
            device_id=to, device_id_type=MESH_ID,
        )
        copy.start()
        return copy

    edges = (edge_send, edge_recv)
    mains = (main_send, main_recv)
    halos = (halo_send, halo_recv)
    edge_copies = [
        send(cl_ref.at[:, 0:128], gl_ref.at[c, :, 2048:2176], edges, 0, ((r + 7) % 8, c)),
        send(cl_ref.at[:, 1920:2048], gl_ref.at[c, :, 2176:2304], edges, 1, ((r + 1) % 8, c)),
        send(cr_ref.at[:, 0:128], gr_ref.at[r, :, 1024:1152], edges, 2, (r, (c + 15) % 16)),
        send(cr_ref.at[:, 896:1024], gr_ref.at[r, :, 1152:1280], edges, 3, (r, (c + 1) % 16)),
    ]
    main_copies = [
        send(cl_ref, gl_ref.at[c, :, 0:2048], mains, d, (r, (c + d) % 16)) for d in range(1, 16)
    ] + [
        send(cr_ref, gr_ref.at[r, :, 0:1024], mains, 15 + d, ((r + d) % 8, c)) for d in range(1, 8)
    ]
    gl_ref[c, :, 0:2048] = cl_ref[...]
    gr_ref[r, :, 0:1024] = cr_ref[...]
    for copy in edge_copies:
        copy.wait()
    halo_copies = [
        send(gl_ref.at[c, :, 2048:2304], gl_ref.at[c, :, 2048:2304], halos, d, (r, (c + d) % 16))
        for d in range(1, 16)
    ] + [
        send(gr_ref.at[r, :, 1024:1280], gr_ref.at[r, :, 1024:1280], halos, 15 + d, ((r + d) % 8, c))
        for d in range(1, 8)
    ]
    for copy in main_copies:
        copy.wait()
    for copy in halo_copies:
        copy.wait()

    @pl.when(r == 0)
    def _():
        gl_ref[:, :, 2176:2304] = jnp.zeros((16, 2, 128), f32)

    @pl.when(r == 7)
    def _():
        gl_ref[:, :, 2048:2176] = jnp.zeros((16, 2, 128), f32)

    @pl.when(c == 0)
    def _():
        gr_ref[:, :, 1152:1280] = jnp.zeros((8, 4, 128), f32)

    @pl.when(c == 15)
    def _():
        gr_ref[:, :, 1024:1152] = jnp.zeros((8, 4, 128), f32)


PIECES = 2


def reduce_grads(
    r, c, gl_ref, gr_ref, ol_ref, or_ref,
    pair_ref, sum_ref, ly_ref, lsum_ref, lz_ref, rx_ref, rsum_ref, rz_ref, sends, recvs,
):
    zlo, x = r // 4, r % 4
    zhi, y, core = c // 8, (c // 2) % 4, c % 2
    pair = (r, c + 1 - 2 * core)
    y_peer = [(r, zhi * 8 + ((y + d) % 4) * 2 + core) for d in range(1, 4)]
    x_peer = [(zlo * 4 + (x + d) % 4, c) for d in range(1, 4)]
    left_z = (r, (c + 8) % 16)
    right_z = ((r + 4) % 8, c)
    rows = 128 // PIECES

    def send(src, dst, at, to):
        copy = pltpu.make_async_remote_copy(
            src_ref=src, dst_ref=dst, send_sem=sends.at[at], recv_sem=recvs.at[at],
            device_id=to, device_id_type=MESH_ID,
        )
        copy.start()
        return copy

    cut = [pl.ds(p * rows, rows) for p in range(PIECES)]
    to_pair = [
        send(gl_ref.at[pl.ds((1 - core) * 8, 8), cut[p]], pair_ref.at[:, cut[p]], p * 9, pair)
        for p in range(PIECES)
    ]
    to_x = [
        [
            send(
                gr_ref.at[pl.ds(((x + d) % 4) * 2, 2), cut[p]], rx_ref.at[d - 1, :, cut[p]],
                p * 9 + d, x_peer[d - 1],
            )
            for d in range(1, 4)
        ]
        for p in range(PIECES)
    ]
    to_y = []
    for p in range(PIECES):
        to_pair[p].wait()
        for s in range(8):
            sum_ref[s, cut[p]] = gl_ref[core * 8 + s, cut[p]] + pair_ref[s, cut[p]]
        to_y.append([
            send(
                sum_ref.at[pl.ds(((y + d) % 4) * 2, 2), cut[p]], ly_ref.at[d - 1, :, cut[p]],
                p * 9 + 3 + d, y_peer[d - 1],
            )
            for d in range(1, 4)
        ])
    to_rz, to_lz = [], []
    for p in range(PIECES):
        for copy in to_x[p]:
            copy.wait()
        for s in range(2):
            rsum_ref[s, cut[p]] = gr_ref[x * 2 + s, cut[p]] + (
                rx_ref[0, s, cut[p]] + rx_ref[1, s, cut[p]] + rx_ref[2, s, cut[p]]
            )
        to_rz.append(send(rsum_ref.at[1 - zlo, cut[p]], rz_ref.at[cut[p]], p * 9 + 7, right_z))
        for copy in to_y[p]:
            copy.wait()
        for s in range(2):
            lsum_ref[s, cut[p]] = sum_ref[y * 2 + s, cut[p]] + (
                ly_ref[0, s, cut[p]] + ly_ref[1, s, cut[p]] + ly_ref[2, s, cut[p]]
            )
        to_lz.append(send(lsum_ref.at[1 - zhi, cut[p]], lz_ref.at[cut[p]], p * 9 + 8, left_z))
    for p in range(PIECES):
        to_rz[p].wait()
        or_ref[cut[p]] = rsum_ref[zlo, cut[p]] + rz_ref[cut[p]]
        to_lz[p].wait()
        ol_ref[cut[p]] = lsum_ref[zhi, cut[p]] + lz_ref[cut[p]]


def step_kernel(
    mask_ref, cl_ref, cr_ref, sl_ref, wl_ref, sr_ref, wr_ref, rows_ref, cols_ref, vals_ref,
    ol_ref, or_ref,
    gl_ref, gr_ref, fl_ref, fr_ref, wl6_ref, wr6_ref, vl_ref, vr_ref, pl_ref, pr_ref,
    pair_ref, sum_ref, ly_ref, lsum_ref, lz_ref, rx_ref, rsum_ref, rz_ref,
    edge_send, edge_recv, main_send, main_recv, halo_send, halo_recv, sends, recvs,
):
    r = lax.axis_index("row")
    c = lax.axis_index("col")
    greet([(r, (c + d) % 16) for d in range(1, 16)] + [((r + d) % 8, c) for d in range(1, 8)])
    gather_coarse(
        r, c, cl_ref, cr_ref, gl_ref, gr_ref, edge_send, edge_recv, main_send, main_recv, halo_send, halo_recv
    )
    spread_weights(sl_ref, wl_ref, wl6_ref, r * 2048, 8192)
    spread_weights(sr_ref, wr_ref, wr6_ref, c * 1024, 4096)

    def local(up_ref, lhs_ref, table_ref):
        upsample_matrix(up_ref)
        coarse_windows(lambda b: gl_ref[:, :, lanes(b * 128)].reshape(32, 128), lhs_ref, 0, LEFT_STEPS)
        coarse_windows(
            lambda b: gr_ref[:, :, lanes(b * 128)].reshape(32, 128), lhs_ref, LEFT_STEPS * 64, RIGHT_STEPS
        )
        interpolate(lhs_ref, up_ref, wl6_ref, fl_ref, 0, LEFT_STEPS)
        interpolate(lhs_ref, up_ref, wr6_ref, fr_ref, LEFT_STEPS * 64, RIGHT_STEPS)
        pl_ref[...] = jnp.zeros(pl_ref.shape, f32)
        pr_ref[...] = jnp.zeros(pr_ref.shape, f32)
        add_own(fl_ref, pl_ref, c, 2, left_place)
        add_own(fr_ref, pr_ref, r, 4, right_place)
        build_table(fr_ref, table_ref)

        def sample(blk):
            sample_block(blk, fl_ref, table_ref, vl_ref, vr_ref, rows_ref, cols_ref, vals_ref, mask_ref)

        def scatter(blk):
            scatter_block(blk, vl_ref, rows_ref, pl_ref, 2, left_place, blk // PER_TILE * 64)
            scatter_block(blk, vr_ref, cols_ref, pr_ref, 4, right_place, 0)

        sample(0)

        @pl.loop(1, BLOCKS)
        def _(blk):
            scatter(blk - 1)
            sample(blk)

        scatter(BLOCKS - 1)

    pl.run_scoped(
        local,
        pltpu.VMEM((256, 1536), bf16),
        pltpu.VMEM(((LEFT_STEPS + RIGHT_STEPS) * 64, 256), bf16),
        pltpu.VMEM((512, 512), bf16),
    )
    reduce_grads(
        r, c, pl_ref, pr_ref, ol_ref, or_ref,
        pair_ref, sum_ref, ly_ref, lsum_ref, lz_ref, rx_ref, rsum_ref, rz_ref, sends, recvs,
    )


def on_device(coarse_left, coarse_right, sl, wl, sr, wr, mask, rows, cols, vals):
    vmem = pl.BlockSpec(memory_space=pltpu.VMEM)
    smem = pl.BlockSpec(memory_space=pltpu.SMEM)
    dma = pltpu.SemaphoreType.DMA
    block = (128, 128)
    left_sum, right_sum = pl.pallas_call(
        step_kernel,
        out_shape=(jax.ShapeDtypeStruct(block, f32), jax.ShapeDtypeStruct(block, f32)),
        in_specs=[smem] + [vmem] * 9,
        out_specs=(vmem, vmem),
        scratch_shapes=[
            pltpu.VMEM((16, 2, 2304), f32),
            pltpu.VMEM((8, 4, 1280), f32),
            pltpu.VMEM((32, 512 * LEFT_STEPS), f32),
            pltpu.VMEM((32, 512 * RIGHT_STEPS), f32),
            pltpu.VMEM((8, 512 * LEFT_STEPS), f32),
            pltpu.VMEM((8, 512 * RIGHT_STEPS), f32),
            pltpu.VMEM((32, 2 * SPT), f32),
            pltpu.VMEM((32, 2 * SPT), f32),
            pltpu.VMEM((16, *block), f32),
            pltpu.VMEM((8, *block), f32),
            pltpu.VMEM((8, *block), f32),
            pltpu.VMEM((8, *block), f32),
            pltpu.VMEM((3, 2, *block), f32),
            pltpu.VMEM((2, *block), f32),
            pltpu.VMEM(block, f32),
            pltpu.VMEM((3, 2, *block), f32),
            pltpu.VMEM((2, *block), f32),
            pltpu.VMEM(block, f32),
            dma((4,)), dma((4,)), dma((23,)), dma((23,)), dma((23,)), dma((23,)),
            dma((9 * PIECES,)), dma((9 * PIECES,)),
        ],
        compiler_params=pltpu.CompilerParams(collective_id=0, has_side_effects=True),
        name="fused_step",
    )(
        mask.reshape(1, 2), coarse_left, coarse_right, sl.reshape(1, -1), wl, sr.reshape(1, -1), wr,
        rows, cols, vals,
    )
    left_new = left_sum.reshape(64, 2, 128).transpose(1, 0, 2).reshape(2, 8192)
    right_new = right_sum.reshape(32, 4, 128).transpose(1, 0, 2).reshape(4, 4096)
    return left_new, right_new


def solution(mesh):
    in_specs = (
        P("col", "row"),
        P("row", "col"),
        P("row"),
        P(None, "row"),
        P("col"),
        P(None, "col"),
        P("row", "col"),
        P("row", "col", None),
        P("row", "col", None),
        P("row", "col", None),
    )
    out_specs = (P("col", "row"), P("row", "col"))
    return jax.shard_map(
        on_device, mesh=mesh, in_specs=in_specs, out_specs=out_specs, check_vma=False
    )
```

```python
import functools
import jax, jax.numpy as jnp
from jax import lax
from jax.sharding import PartitionSpec as P
from jax.experimental import pallas as pl
from jax.experimental.pallas import tpu as pltpu

TILE = 4096
SPT = 2048
BLOCK = 512
BLOCKS = 2 * SPT // BLOCK
PER_TILE = SPT // BLOCK
ETA = 0.5
f32, bf16, i32 = jnp.float32, jnp.bfloat16, jnp.int32


def lanes(at, size=128):
    return pl.ds(pl.multiple_of(at, 128), size)


def lane_pick(table, index):
    return jnp.take_along_axis(table, index, axis=1)


LEFT_STEPS, RIGHT_STEPS = 17, 9
PAD = 384


def upsample_matrix(up_ref):
    row = lax.broadcasted_iota(i32, (16, 128), 0)
    lane = lax.broadcasted_iota(i32, (16, 128), 1)
    for pattern in range(2):
        for offset in range(6):
            gap = (32 * pattern + 30 + offset + (lane >> 2) - row).astype(f32).astype(bf16)
            one, zero = jnp.ones((16, 128), bf16), jnp.zeros((16, 128), bf16)
            for m in range(8):
                part = jnp.where(gap == jnp.full((16, 128), 16 * m, bf16), one, zero)
                at = (pattern * 6 + offset) * 128
                up_ref[16 * m : 16 * m + 16, at : at + 128] = part
                up_ref[128 + 16 * m : 144 + 16 * m, at : at + 128] = part


def spread_weights(stencil_ref, weight_ref, by_offset_ref, origin, count):
    row = lax.broadcasted_iota(i32, (8, 128), 0)
    lane = lax.broadcasted_iota(i32, (8, 128), 1)

    def step(block, _):
        weight = jnp.concatenate(
            [weight_ref[:, lanes(block * 128)], jnp.zeros((4, 128), f32)], axis=0
        )
        stencil = jnp.broadcast_to(stencil_ref[:, lanes(block * 128)], (8, 128))
        base = stencil - (origin + block * 32) - (lane >> 2)
        by_offset_ref[:, lanes(block * 128 + PAD)] = jnp.take_along_axis(
            weight, (row - 1 - base) & 7, axis=0
        )
        return 0

    lax.fori_loop(0, count // 128, step, 0, unroll=4)


def two_terms(value):
    top = value.astype(bf16)
    return top, (value - top.astype(f32)).astype(bf16)


def coarse_windows(coarse, lhs_ref, base, steps):
    def step(b, _):
        here = coarse((b + steps) % (steps + 1))
        after = coarse(b)
        mid = jnp.concatenate([here[:, 64:], after[:, :64]], axis=1)
        for w, window in enumerate((here, mid)):
            top, rest = two_terms(window)
            rows = pl.ds(pl.multiple_of(base + b * 64 + w * 32, 32), 32)
            lhs_ref[rows, 0:128] = top
            lhs_ref[rows, 128:256] = rest
        return 0

    lax.fori_loop(0, steps, step, 0)


def interpolate(lhs_ref, up_ref, by_offset_ref, fine_ref, base, steps):
    for tile in range(6):
        pattern, first = tile // 3, tile % 3 * 2
        got = jnp.dot(
            lhs_ref[base : base + steps * 64, :],
            up_ref[:, tile * 256 : tile * 256 + 256],
            preferred_element_type=f32,
        )
        for b in range(steps):
            for w in range(2):
                at = slice(b * 512 + (2 * w + pattern) * 128, b * 512 + (2 * w + pattern) * 128 + 128)
                weight = [
                    jnp.broadcast_to(by_offset_ref[first + n : first + n + 1, at], (8, 128))
                    for n in range(2)
                ]
                for g in range(4):
                    row = b * 64 + w * 32 + g * 8
                    part = got[row : row + 8, 0:128] * weight[0] + got[row : row + 8, 128:256] * weight[1]
                    if first:
                        part = part + fine_ref[8 * g : 8 * g + 8, at]
                    fine_ref[8 * g : 8 * g + 8, at] = part


def pick_columns(fine_ref, start, position):
    j = jnp.broadcast_to(position >> 7, (8, 128))
    lo = jnp.broadcast_to(position & 127, (8, 128))
    bits = [(j & (1 << b)) != 0 for b in range(5)]

    def tree(g, prefix, bit):
        if bit < 0:
            return lane_pick(fine_ref[8 * g : 8 * g + 8, lanes(PAD + start + prefix * 128)], lo)
        off = tree(g, prefix, bit - 1)
        on = tree(g, prefix | 1 << bit, bit - 1)
        return jnp.where(bits[bit], on, off)

    return [tree(g, 0, 4) for g in range(4)]


def build_table(fine_ref, table_ref):
    def step(hi, _):
        for h in range(2):
            j = (hi >> 1) * 4 + h * 2 + (hi & 1)
            for half in range(2):
                v = fine_ref[16 * half : 16 * half + 16, lanes(PAD + j * 128)]
                top, rest = two_terms(v)
                rows = pl.ds(pl.multiple_of(hi * 32 + 16 * half, 16), 16)
                rest_rows = pl.ds(pl.multiple_of(512 + hi * 32 + 16 * half, 16), 16)
                table_ref[rows, h * 128 : h * 128 + 128] = top
                table_ref[rest_rows, h * 128 : h * 128 + 128] = rest
        return 0

    lax.fori_loop(0, 16, step, 0, unroll=4)


def one_hot(lo):
    lo16 = jnp.broadcast_to(lo, (16, 128)) - lax.broadcasted_iota(i32, (16, 128), 0)
    lo16 = lo16.astype(f32).astype(bf16)
    one, zero = jnp.ones((16, 128), bf16), jnp.zeros((16, 128), bf16)
    return jnp.concatenate(
        [jnp.where(lo16 == jnp.full((16, 128), 16 * m, bf16), one, zero) for m in range(16)], axis=0
    )


def table_columns(table_ref, positions):
    split = [split_position(p, 4) for p in positions]
    hot = jnp.concatenate([one_hot(lo) for _, lo in split], axis=1)
    got = jnp.dot(table_ref[...], hot, preferred_element_type=f32)
    out = []
    for sub, (hi, _) in enumerate(split):
        hi8 = jnp.broadcast_to(hi, (8, 128))
        bits = [(hi8 & (1 << b)) != 0 for b in range(4)]

        def tree(g, prefix, bit):
            if bit < 0:
                row = prefix * 32 + 8 * g
                cut = slice(sub * 128, sub * 128 + 128)
                return got[row : row + 8, cut] + got[512 + row : 520 + row, cut]
            return jnp.where(bits[bit], tree(g, prefix | 1 << bit, bit - 1), tree(g, prefix, bit - 1))

        out.append([tree(g, 0, 3) for g in range(4)])
    return out


def sample_block(blk, fl_ref, table_ref, vl_ref, vr_ref, rows_ref, cols_ref, vals_ref, mask_ref):
    tile = blk // PER_TILE
    subs = [(blk % PER_TILE) * BLOCK + sub * 128 for sub in range(BLOCK // 128)]
    rights = table_columns(table_ref, [cols_ref[tile, :, lanes(at)] for at in subs])
    keep = mask_ref[0, tile].astype(f32) * -ETA
    for sub, at in enumerate(subs):
        left = pick_columns(fl_ref, tile * TILE, rows_ref[tile, :, lanes(at)])
        right = rights[sub]
        dots = (left[0] * right[0] + left[1] * right[1]) + (left[2] * right[2] + left[3] * right[3])
        error = jnp.sum(dots, axis=0, keepdims=True) - vals_ref[tile, :, lanes(at)]
        scaled = jnp.broadcast_to(error * keep, (8, 128))
        out = lanes(blk * BLOCK + sub * 128)
        for g in range(4):
            vl_ref[8 * g : 8 * g + 8, out] = scaled * right[g]
            vr_ref[8 * g : 8 * g + 8, out] = scaled * left[g]


def split_position(position, period):
    half = 8 // period
    j = position >> 7
    hi = (j // (2 * half)) * half + (j & (half - 1))
    lo = ((j // half) & 1) * 128 + (position & 127)
    return hi, lo


def scatter_block(blk, value_ref, position_ref, out_ref, period, place, at, part, parts):
    tile = blk // PER_TILE
    per_tile = 16 // period
    count = 16 // per_tile
    row16 = lax.broadcasted_iota(i32, (16, 128), 0)
    groups = range(4 * part // parts, 4 * (part + 1) // parts)
    hots, columns = [], []
    for sub in range(BLOCK // 128):
        position = position_ref[tile, :, lanes((blk % PER_TILE) * BLOCK + sub * 128)]
        hi, lo = split_position(position, period)
        hi16 = jnp.broadcast_to(hi, (16, 128)) - row16 // period
        masks = [jnp.where(hi16 == m * per_tile, 1.0, 0.0).astype(bf16) for m in range(count)]
        hots.append(one_hot(lo))
        top_rows, rest_rows = [], []
        for g in groups:
            v = value_ref[8 * g : 8 * g + 8, lanes(blk * BLOCK + sub * 128)]
            for first in range(0, 8, period):
                index = first + lax.broadcasted_iota(i32, (8, 128), 0) % period
                dup = jnp.take_along_axis(v, index, axis=0)
                top, rest = two_terms(jnp.concatenate([dup, dup], axis=0))
                top_rows += [top * mask for mask in masks]
                rest_rows += [rest * mask for mask in masks]
        columns.append(jnp.concatenate(top_rows + rest_rows, axis=0))
    lhs = jnp.concatenate(columns, axis=1)
    rhs = jnp.concatenate(hots, axis=1)
    got = lax.dot_general(lhs, rhs, (((1,), (1,)), ((), ())), preferred_element_type=f32)
    slots = 32 // period // parts
    each = 64 * period // 32
    for slot in range(slots):
        for g in range(each):
            for h in range(2):
                row = (slot * each + g) * 8
                cut = slice(h * 128, h * 128 + 128)
                rows = pl.ds(pl.multiple_of(at + g * 16 + h * 8, 8), 8)
                both = got[row : row + 8, cut] + got[512 // parts + row : 512 // parts + row + 8, cut]
                out_ref[place(part * slots + slot), rows, :] += both


def left_place(slot):
    return slot % 2 * 8 + slot // 2 % 4 * 2 + slot // 8


def right_place(slot):
    return slot


def add_own(fine_ref, out_ref, slot, period, place):
    group = pl.multiple_of((slot * period) // 8 * 8, 8)
    row = lax.broadcasted_iota(i32, (8, 128), 0)
    index = (slot * period) % 8 + row % period
    spread = 8 // period

    def step(block, _):
        got = None
        for q in range(spread):
            tall = fine_ref[pl.ds(group, 8), lanes(PAD + (block * spread + q) * 128)]
            picked = jnp.take_along_axis(tall, index, axis=0)
            got = picked if got is None else jnp.where(row // period == q, picked, got)
        out_ref[place(slot), pl.ds(pl.multiple_of(block * 8, 8), 8), :] = got
        return 0

    lax.fori_loop(0, 16, step, 0, unroll=4)


MESH_ID = pl.DeviceIdType.MESH


def gather_coarse(r, c, cl_ref, cr_ref, gl_ref, gr_ref, edges, mains, halos):
    def send(src, dst, sems, at, to):
        return pltpu.make_async_remote_copy(
            src_ref=src, dst_ref=dst, send_sem=sems[0].at[at], recv_sem=sems[1].at[at],
            device_id=to, device_id_type=MESH_ID,
        )

    col_peers = [(d, (r, (c + d) % 16)) for d in range(1, 16)]
    row_peers = [(15 + d, ((r + d) % 8, c)) for d in range(1, 8)]
    left_edges = [
        send(cl_ref.at[:, 0:128], gl_ref.at[c, :, 2048:2176], edges, 0, ((r + 7) % 8, c)),
        send(cl_ref.at[:, 1920:2048], gl_ref.at[c, :, 2176:2304], edges, 1, ((r + 1) % 8, c)),
    ]
    right_edges = [
        send(cr_ref.at[:, 0:128], gr_ref.at[r, :, 1024:1152], edges, 2, (r, (c + 15) % 16)),
        send(cr_ref.at[:, 896:1024], gr_ref.at[r, :, 1152:1280], edges, 3, (r, (c + 1) % 16)),
    ]
    left_mains = [send(cl_ref, gl_ref.at[c, :, 0:2048], mains, at, to) for at, to in col_peers]
    right_mains = [send(cr_ref, gr_ref.at[r, :, 0:1024], mains, at, to) for at, to in row_peers]
    own_left, own_right = gl_ref.at[c, :, 2048:2304], gr_ref.at[r, :, 1024:1280]
    left_halos = [send(own_left, own_left, halos, at, to) for at, to in col_peers]
    right_halos = [send(own_right, own_right, halos, at, to) for at, to in row_peers]

    def begin():
        for copy in left_edges + right_edges + right_mains + left_mains:
            copy.start()
        gl_ref[c, :, 0:2048] = cl_ref[...]
        gr_ref[r, :, 0:1024] = cr_ref[...]

    def forward():
        for copy in right_edges:
            copy.wait()
        for copy in right_halos:
            copy.start()
        for copy in left_edges:
            copy.wait()
        for copy in left_halos:
            copy.start()

    def end_right():
        for copy in right_mains + right_halos:
            copy.wait()

        @pl.when(c == 0)
        def _():
            gr_ref[:, :, 1152:1280] = jnp.zeros((8, 4, 128), f32)

        @pl.when(c == 15)
        def _():
            gr_ref[:, :, 1024:1152] = jnp.zeros((8, 4, 128), f32)

    def end_left():
        for copy in left_mains + left_halos:
            copy.wait()

        @pl.when(r == 0)
        def _():
            gl_ref[:, :, 2176:2304] = jnp.zeros((16, 2, 128), f32)

        @pl.when(r == 7)
        def _():
            gl_ref[:, :, 2048:2176] = jnp.zeros((16, 2, 128), f32)

    return begin, forward, end_right, end_left


class Exchange:
    def __init__(self, r, c, pl_ref, pr_ref, la_ref, lb_ref, ra_ref, rb_ref, work, sends, recvs):
        self.pair_ref, self.sum_ref, self.ly_ref, self.lsum_ref, self.rx_ref, self.rsum_ref = work
        self.pl_ref, self.pr_ref = pl_ref, pr_ref
        self.la_ref, self.lb_ref, self.ra_ref, self.rb_ref = la_ref, lb_ref, ra_ref, rb_ref
        self.sends, self.recvs = sends, recvs
        self.zlo, self.x = r // 4, r % 4
        self.zhi, self.y, self.core = c // 8, (c // 2) % 4, c % 2
        self.r, self.c = r, c

    def send(self, src, dst, at, to):
        return pltpu.make_async_remote_copy(
            src_ref=src, dst_ref=dst, send_sem=self.sends.at[at], recv_sem=self.recvs.at[at],
            device_id=to, device_id_type=MESH_ID,
        )

    def pair(self, p):
        cut = pl.ds(p * 64, 64)
        return self.send(
            self.pl_ref.at[pl.ds((1 - self.core) * 8, 8), cut], self.pair_ref.at[:, cut], p,
            (self.r, self.c + 1 - 2 * self.core),
        )

    def along_y(self, p):
        cut = pl.ds(p * 64, 64)
        out = []
        for d in range(1, 4):
            there = (self.y + d) % 4
            out.append(self.send(
                self.sum_ref.at[pl.ds(there * 2, 2), cut], self.ly_ref.at[d - 1, :, cut],
                2 + p * 3 + d - 1, (self.r, self.zhi * 8 + there * 2 + self.core),
            ))
        return out

    def left_z(self, p):
        cut = pl.ds(p * 64, 64)
        return self.send(
            self.lsum_ref.at[1 - self.zhi, cut], self.lb_ref.at[cut], 8 + p, (self.r, (self.c + 8) % 16)
        )

    def along_x(self, half):
        out = []
        for d in range(1, 4):
            there = (self.x + d) % 4
            out.append(self.send(
                self.pr_ref.at[half * 4 + there], self.rx_ref.at[half, d - 1],
                10 + half * 3 + d - 1, (self.zlo * 4 + there, self.c),
            ))
        return out

    def right_z(self):
        return self.send(
            self.rsum_ref.at[1 - self.zlo], self.rb_ref, 16, ((self.r + 4) % 8, self.c)
        )

    def after_pair(self, p):
        cut = pl.ds(p * 64, 64)
        self.pair(p).wait()
        for s in range(8):
            self.sum_ref[s, cut] = self.pl_ref[self.core * 8 + s, cut] + self.pair_ref[s, cut]
        for copy in self.along_y(p):
            copy.start()

    def after_y(self, p):
        cut = pl.ds(p * 64, 64)
        for copy in self.along_y(p):
            copy.wait()
        for s in range(2):
            self.lsum_ref[s, cut] = self.sum_ref[self.y * 2 + s, cut] + (
                self.ly_ref[0, s, cut] + self.ly_ref[1, s, cut] + self.ly_ref[2, s, cut]
            )
        self.left_z(p).start()

    def after_x(self, half):
        for copy in self.along_x(half):
            copy.wait()
        self.rsum_ref[half] = self.pr_ref[half * 4 + self.x] + (
            self.rx_ref[half, 0] + self.rx_ref[half, 1] + self.rx_ref[half, 2]
        )

        @pl.when(self.zlo == 1 - half)
        def _():
            self.right_z().start()

    def end(self):
        self.la_ref[...] = self.lsum_ref[self.zhi]
        self.ra_ref[...] = self.rsum_ref[self.zlo]
        self.right_z().wait()
        for p in range(2):
            self.left_z(p).wait()


def step_kernel(
    mask_ref, cl_ref, cr_ref, sl_ref, wl_ref, sr_ref, wr_ref, rows_ref, cols_ref, vals_ref,
    la_ref, lb_ref, ra_ref, rb_ref,
    gl_ref, gr_ref, fl_ref, fr_ref, wl6_ref, wr6_ref, vl_ref, vr_ref, pl_ref, pr_ref,
    pair_ref, sum_ref, ly_ref, lsum_ref, rx_ref, rsum_ref,
    edge_send, edge_recv, main_send, main_recv, halo_send, halo_recv, sends, recvs,
):
    r = lax.axis_index("row")
    c = lax.axis_index("col")
    peers = [(r, (c + d) % 16) for d in range(1, 16)] + [((r + d) % 8, c) for d in range(1, 8)]
    barrier = pltpu.get_barrier_semaphore()
    for peer in peers:
        pl.semaphore_signal(barrier, inc=1, device_id=peer, device_id_type=MESH_ID)
    begin, forward, end_right, end_left = gather_coarse(
        r, c, cl_ref, cr_ref, gl_ref, gr_ref,
        (edge_send, edge_recv), (main_send, main_recv), (halo_send, halo_recv),
    )
    exchange = Exchange(
        r, c, pl_ref, pr_ref, la_ref, lb_ref, ra_ref, rb_ref,
        (pair_ref, sum_ref, ly_ref, lsum_ref, rx_ref, rsum_ref), sends, recvs,
    )

    def local(up_ref, lhs_ref, table_ref):
        spread_weights(sr_ref, wr_ref, wr6_ref, c * 1024, 4096)
        upsample_matrix(up_ref)
        pl.semaphore_wait(barrier, len(peers))
        begin()
        spread_weights(sl_ref, wl_ref, wl6_ref, r * 2048, 8192)
        forward()
        pl_ref[...] = jnp.zeros(pl_ref.shape, f32)
        pr_ref[...] = jnp.zeros(pr_ref.shape, f32)
        end_right()
        right_base = LEFT_STEPS * 64
        coarse_windows(
            lambda b: gr_ref[:, :, lanes(b * 128)].reshape(32, 128), lhs_ref, right_base, RIGHT_STEPS
        )
        interpolate(lhs_ref, up_ref, wr6_ref, fr_ref, right_base, RIGHT_STEPS)
        build_table(fr_ref, table_ref)
        add_own(fr_ref, pr_ref, r, 4, right_place)
        end_left()
        coarse_windows(lambda b: gl_ref[:, :, lanes(b * 128)].reshape(32, 128), lhs_ref, 0, LEFT_STEPS)
        interpolate(lhs_ref, up_ref, wl6_ref, fl_ref, 0, LEFT_STEPS)
        add_own(fl_ref, pl_ref, c, 2, left_place)

        def sample(blk):
            sample_block(blk, fl_ref, table_ref, vl_ref, vr_ref, rows_ref, cols_ref, vals_ref, mask_ref)

        def scatter_left(blk):
            scatter_block(blk, vl_ref, rows_ref, pl_ref, 2, left_place, blk // PER_TILE * 64, 0, 1)

        sample(0)

        @pl.loop(1, BLOCKS)
        def _(blk):
            scatter_left(blk - 1)
            sample(blk)

            @pl.when(blk == PER_TILE)
            def _():
                exchange.pair(0).start()

            @pl.when(blk == PER_TILE + 2)
            def _():
                exchange.after_pair(0)

        scatter_left(BLOCKS - 1)
        exchange.pair(1).start()

        @pl.loop(0, BLOCKS)
        def _(blk):
            scatter_block(blk, vr_ref, cols_ref, pr_ref, 4, right_place, 0, 0, 2)

            @pl.when(blk == BLOCKS - 1)
            def _():
                exchange.after_pair(1)

        for copy in exchange.along_x(0):
            copy.start()

        @pl.loop(0, BLOCKS)
        def _(blk):
            scatter_block(blk, vr_ref, cols_ref, pr_ref, 4, right_place, 0, 1, 2)

            @pl.when(blk == BLOCKS // 2)
            def _():
                exchange.after_y(0)

        for copy in exchange.along_x(1):
            copy.start()
        exchange.after_x(0)
        exchange.after_y(1)
        exchange.after_x(1)
        exchange.end()

    pl.run_scoped(
        local,
        pltpu.VMEM((256, 1536), bf16),
        pltpu.VMEM(((LEFT_STEPS + RIGHT_STEPS) * 64, 256), bf16),
        pltpu.VMEM((1024, 256), bf16),
    )


def on_device(coarse_left, coarse_right, sl, wl, sr, wr, mask, rows, cols, vals):
    vmem = pl.BlockSpec(memory_space=pltpu.VMEM)
    smem = pl.BlockSpec(memory_space=pltpu.SMEM)
    dma = pltpu.SemaphoreType.DMA
    block = (128, 128)
    la, lb, ra, rb = pl.pallas_call(
        step_kernel,
        out_shape=(jax.ShapeDtypeStruct(block, f32),) * 4,
        in_specs=[smem] + [vmem] * 9,
        out_specs=(vmem,) * 4,
        scratch_shapes=[
            pltpu.VMEM((16, 2, 2304), f32),
            pltpu.VMEM((8, 4, 1280), f32),
            pltpu.VMEM((32, 512 * LEFT_STEPS), f32),
            pltpu.VMEM((32, 512 * RIGHT_STEPS), f32),
            pltpu.VMEM((8, 512 * LEFT_STEPS), f32),
            pltpu.VMEM((8, 512 * RIGHT_STEPS), f32),
            pltpu.VMEM((32, 2 * SPT), f32),
            pltpu.VMEM((32, 2 * SPT), f32),
            pltpu.VMEM((16, *block), f32),
            pltpu.VMEM((8, *block), f32),
            pltpu.VMEM((8, *block), f32),
            pltpu.VMEM((8, *block), f32),
            pltpu.VMEM((3, 2, *block), f32),
            pltpu.VMEM((2, *block), f32),
            pltpu.VMEM((2, 3, *block), f32),
            pltpu.VMEM((2, *block), f32),
            dma((4,)), dma((4,)), dma((23,)), dma((23,)), dma((23,)), dma((23,)),
            dma((17,)), dma((17,)),
        ],
        compiler_params=pltpu.CompilerParams(collective_id=0, has_side_effects=True),
        name="fused_step",
    )(
        mask.reshape(1, 2), coarse_left, coarse_right, sl.reshape(1, -1), wl, sr.reshape(1, -1), wr,
        rows, cols, vals,
    )
    left_new = (la + lb).reshape(64, 2, 128).transpose(1, 0, 2).reshape(2, 8192)
    right_new = (ra + rb).reshape(32, 4, 128).transpose(1, 0, 2).reshape(4, 4096)
    return left_new, right_new


def solution(mesh):
    in_specs = (
        P("col", "row"),
        P("row", "col"),
        P("row"),
        P(None, "row"),
        P("col"),
        P(None, "col"),
        P("row", "col"),
        P("row", "col", None),
        P("row", "col", None),
        P("row", "col", None),
    )
    out_specs = (P("col", "row"), P("row", "col"))
    return jax.shard_map(
        on_device, mesh=mesh, in_specs=in_specs, out_specs=out_specs, check_vma=False
    )
```

```python
import functools
import jax, jax.numpy as jnp
from jax import lax
from jax.sharding import PartitionSpec as P
from jax.experimental import pallas as pl
from jax.experimental.pallas import tpu as pltpu

TILE = 4096
SPT = 2048
BLOCK = 512
BLOCKS = 2 * SPT // BLOCK
PER_TILE = SPT // BLOCK
ETA = 0.5
f32, bf16, i32 = jnp.float32, jnp.bfloat16, jnp.int32


def lanes(at, size=128):
    return pl.ds(pl.multiple_of(at, 128), size)


def lane_pick(table, index):
    return jnp.take_along_axis(table, index, axis=1)


LEFT_STEPS, RIGHT_STEPS = 17, 9
PAD = 384


def upsample_matrix(up_ref):
    row = lax.broadcasted_iota(i32, (16, 128), 0)
    lane = lax.broadcasted_iota(i32, (16, 128), 1)
    for pattern in range(2):
        for offset in range(6):
            gap = (32 * pattern + 30 + offset + (lane >> 2) - row).astype(f32).astype(bf16)
            one, zero = jnp.ones((16, 128), bf16), jnp.zeros((16, 128), bf16)
            for m in range(8):
                part = jnp.where(gap == jnp.full((16, 128), 16 * m, bf16), one, zero)
                at = (pattern * 6 + offset) * 128
                up_ref[16 * m : 16 * m + 16, at : at + 128] = part
                up_ref[128 + 16 * m : 144 + 16 * m, at : at + 128] = part


def spread_weights(stencil_ref, weight_ref, by_offset_ref, origin, count):
    row = lax.broadcasted_iota(i32, (8, 128), 0)
    lane = lax.broadcasted_iota(i32, (8, 128), 1)

    def step(block, _):
        weight = jnp.concatenate(
            [weight_ref[:, lanes(block * 128)], jnp.zeros((4, 128), f32)], axis=0
        )
        stencil = jnp.broadcast_to(stencil_ref[:, lanes(block * 128)], (8, 128))
        base = stencil - (origin + block * 32) - (lane >> 2)
        by_offset_ref[:, lanes(block * 128 + PAD)] = jnp.take_along_axis(
            weight, (row - 1 - base) & 7, axis=0
        )
        return 0

    lax.fori_loop(0, count // 128, step, 0, unroll=4)


def two_terms(value):
    top = value.astype(bf16)
    return top, (value - top.astype(f32)).astype(bf16)


def coarse_windows(coarse, lhs_ref, base, steps):
    here = coarse(steps)
    for b in range(steps):
        after = coarse(b)
        mid = jnp.concatenate([here[:, 64:], after[:, :64]], axis=1)
        for w, window in enumerate((here, mid)):
            top, rest = two_terms(window)
            rows = slice(base + b * 64 + w * 32, base + b * 64 + w * 32 + 32)
            lhs_ref[rows, 0:128] = top
            lhs_ref[rows, 128:256] = rest
        here = after


def interpolate(lhs_ref, up_ref, by_offset_ref, fine_ref, base, steps):
    for tile in range(6):
        pattern, first = tile // 3, tile % 3 * 2
        got = jnp.dot(
            lhs_ref[base : base + steps * 64, :],
            up_ref[:, tile * 256 : tile * 256 + 256],
            preferred_element_type=f32,
        )
        for b in range(steps):
            for w in range(2):
                at = slice(b * 512 + (2 * w + pattern) * 128, b * 512 + (2 * w + pattern) * 128 + 128)
                weight = [
                    jnp.broadcast_to(by_offset_ref[first + n : first + n + 1, at], (8, 128))
                    for n in range(2)
                ]
                for g in range(4):
                    row = b * 64 + w * 32 + g * 8
                    part = got[row : row + 8, 0:128] * weight[0] + got[row : row + 8, 128:256] * weight[1]
                    if first:
                        part = part + fine_ref[8 * g : 8 * g + 8, at]
                    fine_ref[8 * g : 8 * g + 8, at] = part


def pick_columns(fine_ref, start, position):
    j = jnp.broadcast_to(position >> 7, (8, 128))
    lo = jnp.broadcast_to(position & 127, (8, 128))
    bits = [(j & (1 << b)) != 0 for b in range(5)]

    def tree(g, prefix, bit):
        if bit < 0:
            return lane_pick(fine_ref[8 * g : 8 * g + 8, lanes(PAD + start + prefix * 128)], lo)
        off = tree(g, prefix, bit - 1)
        on = tree(g, prefix | 1 << bit, bit - 1)
        return jnp.where(bits[bit], on, off)

    return [tree(g, 0, 4) for g in range(4)]


def build_table(fine_ref, table_ref):
    def step(hi, _):
        for h in range(2):
            j = (hi >> 1) * 4 + h * 2 + (hi & 1)
            for half in range(2):
                v = fine_ref[16 * half : 16 * half + 16, lanes(PAD + j * 128)]
                top, rest = two_terms(v)
                rows = pl.ds(pl.multiple_of(hi * 32 + 16 * half, 16), 16)
                rest_rows = pl.ds(pl.multiple_of(512 + hi * 32 + 16 * half, 16), 16)
                table_ref[rows, h * 128 : h * 128 + 128] = top
                table_ref[rest_rows, h * 128 : h * 128 + 128] = rest
        return 0

    lax.fori_loop(0, 16, step, 0, unroll=4)


def one_hot(lo):
    lo16 = jnp.broadcast_to(lo, (16, 128)) - lax.broadcasted_iota(i32, (16, 128), 0)
    lo16 = lo16.astype(f32).astype(bf16)
    one, zero = jnp.ones((16, 128), bf16), jnp.zeros((16, 128), bf16)
    return jnp.concatenate(
        [jnp.where(lo16 == jnp.full((16, 128), 16 * m, bf16), one, zero) for m in range(16)], axis=0
    )


def index_tables(position_ref, hot_ref, hi_ref, period):
    per_tile = 16 // period
    row16 = lax.broadcasted_iota(i32, (16, 128), 0)

    for tile in range(2):
        def step(n, _):
            hi, lo = split_position(position_ref[tile, :, lanes(n * 128)], period)
            at = lanes(tile * SPT + n * 128)
            hot_ref[:, at] = one_hot(lo)
            hi16 = (jnp.broadcast_to(hi, (16, 128)) - row16 // period).astype(f32).astype(bf16)
            one, zero = jnp.ones((16, 128), bf16), jnp.zeros((16, 128), bf16)
            for m in range(period):
                same = hi16 == jnp.full((16, 128), m * per_tile, bf16)
                hi_ref[16 * m : 16 * m + 16, at] = jnp.where(same, one, zero)
            return 0

        lax.fori_loop(0, SPT // 128, step, 0, unroll=2)


def table_columns(table_ref, hot, positions):
    got = jnp.dot(table_ref[...], hot, preferred_element_type=f32)
    out = []
    for sub, position in enumerate(positions):
        hi, _ = split_position(position, 4)
        hi8 = jnp.broadcast_to(hi, (8, 128))
        bits = [(hi8 & (1 << b)) != 0 for b in range(4)]

        def tree(g, prefix, bit):
            if bit < 0:
                row = prefix * 32 + 8 * g
                cut = slice(sub * 128, sub * 128 + 128)
                return got[row : row + 8, cut] + got[512 + row : 520 + row, cut]
            return jnp.where(bits[bit], tree(g, prefix | 1 << bit, bit - 1), tree(g, prefix, bit - 1))

        out.append([tree(g, 0, 3) for g in range(4)])
    return out


def sample_block(blk, fl_ref, table_ref, hot_ref, vl_ref, vr_ref, rows_ref, cols_ref, vals_ref, mask_ref):
    tile = blk // PER_TILE
    subs = [(blk % PER_TILE) * BLOCK + sub * 128 for sub in range(BLOCK // 128)]
    hot = hot_ref[:, lanes(blk * BLOCK, BLOCK)]
    rights = table_columns(table_ref, hot, [cols_ref[tile, :, lanes(at)] for at in subs])
    keep = mask_ref[0, tile].astype(f32) * -ETA
    for sub, at in enumerate(subs):
        left = pick_columns(fl_ref, tile * TILE, rows_ref[tile, :, lanes(at)])
        right = rights[sub]
        dots = (left[0] * right[0] + left[1] * right[1]) + (left[2] * right[2] + left[3] * right[3])
        error = jnp.sum(dots, axis=0, keepdims=True) - vals_ref[tile, :, lanes(at)]
        scaled = jnp.broadcast_to(error * keep, (8, 128))
        out = lanes(blk * BLOCK + sub * 128)
        for g in range(4):
            vl_ref[8 * g : 8 * g + 8, out] = scaled * right[g]
            vr_ref[8 * g : 8 * g + 8, out] = scaled * left[g]


def split_position(position, period):
    half = 8 // period
    j = position >> 7
    hi = (j // (2 * half)) * half + (j & (half - 1))
    lo = ((j // half) & 1) * 128 + (position & 127)
    return hi, lo


def scatter_block(first_sample, samples, value_ref, hot_ref, hi_ref, out_ref, period, place, at, part, parts):
    groups = range(4 * part // parts, 4 * (part + 1) // parts)
    columns = []
    for sub in range(samples // 128):
        here = lanes(first_sample + sub * 128)
        masks = [hi_ref[16 * m : 16 * m + 16, here] for m in range(period)]
        top_rows, rest_rows = [], []
        for g in groups:
            v = value_ref[8 * g : 8 * g + 8, here]
            for first in range(0, 8, period):
                index = first + lax.broadcasted_iota(i32, (8, 128), 0) % period
                dup = jnp.take_along_axis(v, index, axis=0)
                top, rest = two_terms(jnp.concatenate([dup, dup], axis=0))
                top_rows += [top * mask for mask in masks]
                rest_rows += [rest * mask for mask in masks]
        columns.append(jnp.concatenate(top_rows + rest_rows, axis=0))
    lhs = jnp.concatenate(columns, axis=1)
    rhs = hot_ref[:, lanes(first_sample, samples)]
    got = lax.dot_general(lhs, rhs, (((1,), (1,)), ((), ())), preferred_element_type=f32)
    slots = 32 // period // parts
    each = 64 * period // 32
    for slot in range(slots):
        for g in range(each):
            for h in range(2):
                row = (slot * each + g) * 8
                cut = slice(h * 128, h * 128 + 128)
                rows = pl.ds(pl.multiple_of(at + g * 16 + h * 8, 8), 8)
                both = got[row : row + 8, cut] + got[512 // parts + row : 512 // parts + row + 8, cut]
                out_ref[place(part * slots + slot), rows, :] += both


def left_place(slot):
    return slot % 2 * 8 + slot // 2 % 4 * 2 + slot // 8


def right_place(slot):
    return slot


def add_own(fine_ref, out_ref, slot, period, place):
    group = pl.multiple_of((slot * period) // 8 * 8, 8)
    row = lax.broadcasted_iota(i32, (8, 128), 0)
    index = (slot * period) % 8 + row % period
    spread = 8 // period

    def step(block, _):
        got = None
        for q in range(spread):
            tall = fine_ref[pl.ds(group, 8), lanes(PAD + (block * spread + q) * 128)]
            picked = jnp.take_along_axis(tall, index, axis=0)
            got = picked if got is None else jnp.where(row // period == q, picked, got)
        out_ref[place(slot), pl.ds(pl.multiple_of(block * 8, 8), 8), :] = got
        return 0

    lax.fori_loop(0, 16, step, 0, unroll=4)


MESH_ID = pl.DeviceIdType.MESH


def gather_coarse(r, c, cl_ref, cr_ref, gl_ref, gr_ref, edges, mains, halos):
    def send(src, dst, sems, at, to):
        return pltpu.make_async_remote_copy(
            src_ref=src, dst_ref=dst, send_sem=sems[0].at[at], recv_sem=sems[1].at[at],
            device_id=to, device_id_type=MESH_ID,
        )

    col_peers = [(d, (r, (c + d) % 16)) for d in range(1, 16)]
    row_peers = [(15 + d, ((r + d) % 8, c)) for d in range(1, 8)]
    left_edges = [
        send(cl_ref.at[:, 0:128], gl_ref.at[c, :, 2048:2176], edges, 0, ((r + 7) % 8, c)),
        send(cl_ref.at[:, 1920:2048], gl_ref.at[c, :, 2176:2304], edges, 1, ((r + 1) % 8, c)),
    ]
    right_edges = [
        send(cr_ref.at[:, 0:128], gr_ref.at[r, :, 1024:1152], edges, 2, (r, (c + 15) % 16)),
        send(cr_ref.at[:, 896:1024], gr_ref.at[r, :, 1152:1280], edges, 3, (r, (c + 1) % 16)),
    ]
    left_mains = [send(cl_ref, gl_ref.at[c, :, 0:2048], mains, at, to) for at, to in col_peers]
    right_mains = [send(cr_ref, gr_ref.at[r, :, 0:1024], mains, at, to) for at, to in row_peers]
    own_left, own_right = gl_ref.at[c, :, 2048:2304], gr_ref.at[r, :, 1024:1280]
    left_halos = [send(own_left, own_left, halos, at, to) for at, to in col_peers]
    right_halos = [send(own_right, own_right, halos, at, to) for at, to in row_peers]

    def begin():
        for copy in left_edges + right_edges + right_mains + left_mains:
            copy.start()
        gl_ref[c, :, 0:2048] = cl_ref[...]
        gr_ref[r, :, 0:1024] = cr_ref[...]

    def forward():
        for copy in right_edges:
            copy.wait()
        for copy in right_halos:
            copy.start()
        for copy in left_edges:
            copy.wait()
        for copy in left_halos:
            copy.start()

    def end_right():
        for copy in right_mains + right_halos:
            copy.wait()

        @pl.when(c == 0)
        def _():
            gr_ref[:, :, 1152:1280] = jnp.zeros((8, 4, 128), f32)

        @pl.when(c == 15)
        def _():
            gr_ref[:, :, 1024:1152] = jnp.zeros((8, 4, 128), f32)

    def end_left():
        for copy in left_mains + left_halos:
            copy.wait()

        @pl.when(r == 0)
        def _():
            gl_ref[:, :, 2176:2304] = jnp.zeros((16, 2, 128), f32)

        @pl.when(r == 7)
        def _():
            gl_ref[:, :, 2048:2176] = jnp.zeros((16, 2, 128), f32)

    return begin, forward, end_right, end_left


class Exchange:
    def __init__(self, r, c, pl_ref, pr_ref, la_ref, lb_ref, ra_ref, rb_ref, work, sends, recvs):
        self.pair_ref, self.sum_ref, self.ly_ref, self.lsum_ref, self.rx_ref, self.rsum_ref = work
        self.pl_ref, self.pr_ref = pl_ref, pr_ref
        self.la_ref, self.lb_ref, self.ra_ref, self.rb_ref = la_ref, lb_ref, ra_ref, rb_ref
        self.sends, self.recvs = sends, recvs
        self.zlo, self.x = r // 4, r % 4
        self.zhi, self.y, self.core = c // 8, (c // 2) % 4, c % 2
        self.r, self.c = r, c

    def send(self, src, dst, at, to):
        return pltpu.make_async_remote_copy(
            src_ref=src, dst_ref=dst, send_sem=self.sends.at[at], recv_sem=self.recvs.at[at],
            device_id=to, device_id_type=MESH_ID,
        )

    def pair(self, p):
        cut = pl.ds(p * 64, 64)
        return self.send(
            self.pl_ref.at[pl.ds((1 - self.core) * 8, 8), cut], self.pair_ref.at[:, cut], p,
            (self.r, self.c + 1 - 2 * self.core),
        )

    def along_y(self, p):
        cut = pl.ds(p * 64, 64)
        out = []
        for d in range(1, 4):
            there = (self.y + d) % 4
            out.append(self.send(
                self.sum_ref.at[pl.ds(there * 2, 2), cut], self.ly_ref.at[d - 1, :, cut],
                2 + p * 3 + d - 1, (self.r, self.zhi * 8 + there * 2 + self.core),
            ))
        return out

    def left_z(self, p):
        cut = pl.ds(p * 64, 64)
        return self.send(
            self.lsum_ref.at[1 - self.zhi, cut], self.lb_ref.at[cut], 8 + p, (self.r, (self.c + 8) % 16)
        )

    def along_x(self, half):
        out = []
        for d in range(1, 4):
            there = (self.x + d) % 4
            out.append(self.send(
                self.pr_ref.at[half * 4 + there], self.rx_ref.at[half, d - 1],
                10 + half * 3 + d - 1, (self.zlo * 4 + there, self.c),
            ))
        return out

    def right_z(self):
        return self.send(
            self.rsum_ref.at[1 - self.zlo], self.rb_ref, 16, ((self.r + 4) % 8, self.c)
        )

    def after_pair(self, p):
        cut = pl.ds(p * 64, 64)
        self.pair(p).wait()
        for s in range(8):
            self.sum_ref[s, cut] = self.pl_ref[self.core * 8 + s, cut] + self.pair_ref[s, cut]
        for copy in self.along_y(p):
            copy.start()

    def after_y(self, p):
        cut = pl.ds(p * 64, 64)
        for copy in self.along_y(p):
            copy.wait()
        for s in range(2):
            self.lsum_ref[s, cut] = self.sum_ref[self.y * 2 + s, cut] + (
                self.ly_ref[0, s, cut] + self.ly_ref[1, s, cut] + self.ly_ref[2, s, cut]
            )
        self.left_z(p).start()

    def after_x(self, half):
        for copy in self.along_x(half):
            copy.wait()
        self.rsum_ref[half] = self.pr_ref[half * 4 + self.x] + (
            self.rx_ref[half, 0] + self.rx_ref[half, 1] + self.rx_ref[half, 2]
        )

        @pl.when(self.zlo == 1 - half)
        def _():
            self.right_z().start()

    def end(self):
        self.la_ref[...] = self.lsum_ref[self.zhi]
        self.ra_ref[...] = self.rsum_ref[self.zlo]
        self.right_z().wait()
        for p in range(2):
            self.left_z(p).wait()


def step_kernel(
    mask_ref, cl_ref, cr_ref, sl_ref, wl_ref, sr_ref, wr_ref, rows_ref, cols_ref, vals_ref,
    la_ref, lb_ref, ra_ref, rb_ref,
    gl_ref, gr_ref, fl_ref, fr_ref, wl6_ref, wr6_ref, vl_ref, vr_ref, pl_ref, pr_ref,
    pair_ref, sum_ref, ly_ref, lsum_ref, rx_ref, rsum_ref,
    edge_send, edge_recv, main_send, main_recv, halo_send, halo_recv, sends, recvs,
):
    r = lax.axis_index("row")
    c = lax.axis_index("col")
    peers = [(r, (c + d) % 16) for d in range(1, 16)] + [((r + d) % 8, c) for d in range(1, 8)]
    barrier = pltpu.get_barrier_semaphore()
    for peer in peers:
        pl.semaphore_signal(barrier, inc=1, device_id=peer, device_id_type=MESH_ID)
    begin, forward, end_right, end_left = gather_coarse(
        r, c, cl_ref, cr_ref, gl_ref, gr_ref,
        (edge_send, edge_recv), (main_send, main_recv), (halo_send, halo_recv),
    )
    exchange = Exchange(
        r, c, pl_ref, pr_ref, la_ref, lb_ref, ra_ref, rb_ref,
        (pair_ref, sum_ref, ly_ref, lsum_ref, rx_ref, rsum_ref), sends, recvs,
    )

    def local(up_ref, lhs_ref, table_ref, hotr_ref, hotc_ref, hir_ref, hic_ref):
        spread_weights(sr_ref, wr_ref, wr6_ref, c * 1024, 4096)
        upsample_matrix(up_ref)
        spread_weights(sl_ref, wl_ref, wl6_ref, r * 2048, 8192)
        pl.semaphore_wait(barrier, len(peers))
        begin()
        index_tables(cols_ref, hotc_ref, hic_ref, 4)
        forward()
        index_tables(rows_ref, hotr_ref, hir_ref, 2)
        pl_ref[...] = jnp.zeros(pl_ref.shape, f32)
        pr_ref[...] = jnp.zeros(pr_ref.shape, f32)
        end_right()
        right_base = LEFT_STEPS * 64
        coarse_windows(
            lambda b: gr_ref[:, :, lanes(b * 128)].reshape(32, 128), lhs_ref, right_base, RIGHT_STEPS
        )
        interpolate(lhs_ref, up_ref, wr6_ref, fr_ref, right_base, RIGHT_STEPS)
        build_table(fr_ref, table_ref)
        add_own(fr_ref, pr_ref, r, 4, right_place)
        end_left()
        coarse_windows(lambda b: gl_ref[:, :, lanes(b * 128)].reshape(32, 128), lhs_ref, 0, LEFT_STEPS)
        interpolate(lhs_ref, up_ref, wl6_ref, fl_ref, 0, LEFT_STEPS)
        add_own(fl_ref, pl_ref, c, 2, left_place)

        def sample(blk):
            sample_block(
                blk, fl_ref, table_ref, hotc_ref, vl_ref, vr_ref, rows_ref, cols_ref, vals_ref, mask_ref
            )

        def scatter(blk):
            at = blk // PER_TILE * 64
            scatter_block(
                blk * BLOCK, BLOCK, vl_ref, hotr_ref, hir_ref, pl_ref, 2, left_place, at, 0, 1
            )
            scatter_block(
                blk * BLOCK, BLOCK, vr_ref, hotc_ref, hic_ref, pr_ref, 4, right_place, 0, 0, 2
            )

        sample(0)

        @pl.loop(1, BLOCKS)
        def _(blk):
            scatter(blk - 1)
            sample(blk)

            @pl.when(blk == PER_TILE)
            def _():
                exchange.pair(0).start()

            @pl.when(blk == PER_TILE + 2)
            def _():
                exchange.after_pair(0)

        scatter(BLOCKS - 1)
        exchange.pair(1).start()
        for copy in exchange.along_x(0):
            copy.start()

        @pl.loop(0, BLOCKS // 2)
        def _(step):
            scatter_block(
                step * 2 * BLOCK, 2 * BLOCK, vr_ref, hotc_ref, hic_ref, pr_ref, 4, right_place, 0, 1, 2
            )

            @pl.when(step == BLOCKS // 2 - 1)
            def _():
                exchange.after_pair(1)

        for copy in exchange.along_x(1):
            copy.start()
        exchange.after_y(0)
        exchange.after_x(0)
        exchange.after_y(1)
        exchange.after_x(1)
        exchange.end()

    pl.run_scoped(
        local,
        pltpu.VMEM((256, 1536), bf16),
        pltpu.VMEM(((LEFT_STEPS + RIGHT_STEPS) * 64, 256), bf16),
        pltpu.VMEM((1024, 256), bf16),
        pltpu.VMEM((256, 2 * SPT), bf16),
        pltpu.VMEM((256, 2 * SPT), bf16),
        pltpu.VMEM((32, 2 * SPT), bf16),
        pltpu.VMEM((64, 2 * SPT), bf16),
    )


def finish_kernel(la_ref, lb_ref, ra_ref, rb_ref, left_ref, right_ref):
    left_ref[...] = la_ref[...] + lb_ref[...]
    right_ref[...] = ra_ref[...] + rb_ref[...]


def on_device(coarse_left, coarse_right, sl, wl, sr, wr, mask, rows, cols, vals):
    vmem = pl.BlockSpec(memory_space=pltpu.VMEM)
    smem = pl.BlockSpec(memory_space=pltpu.SMEM)
    dma = pltpu.SemaphoreType.DMA
    block = (128, 128)
    la, lb, ra, rb = pl.pallas_call(
        step_kernel,
        out_shape=(jax.ShapeDtypeStruct(block, f32),) * 4,
        in_specs=[smem] + [vmem] * 9,
        out_specs=(vmem,) * 4,
        scratch_shapes=[
            pltpu.VMEM((16, 2, 2304), f32),
            pltpu.VMEM((8, 4, 1280), f32),
            pltpu.VMEM((32, 512 * LEFT_STEPS), f32),
            pltpu.VMEM((32, 512 * RIGHT_STEPS), f32),
            pltpu.VMEM((8, 512 * LEFT_STEPS), f32),
            pltpu.VMEM((8, 512 * RIGHT_STEPS), f32),
            pltpu.VMEM((32, 2 * SPT), f32),
            pltpu.VMEM((32, 2 * SPT), f32),
            pltpu.VMEM((16, *block), f32),
            pltpu.VMEM((8, *block), f32),
            pltpu.VMEM((8, *block), f32),
            pltpu.VMEM((8, *block), f32),
            pltpu.VMEM((3, 2, *block), f32),
            pltpu.VMEM((2, *block), f32),
            pltpu.VMEM((2, 3, *block), f32),
            pltpu.VMEM((2, *block), f32),
            dma((4,)), dma((4,)), dma((23,)), dma((23,)), dma((23,)), dma((23,)),
            dma((17,)), dma((17,)),
        ],
        compiler_params=pltpu.CompilerParams(collective_id=0, has_side_effects=True),
        name="fused_step",
    )(
        mask.reshape(1, 2), coarse_left, coarse_right, sl.reshape(1, -1), wl, sr.reshape(1, -1), wr,
        rows, cols, vals,
    )
    left_sum, right_sum = pl.pallas_call(
        finish_kernel,
        out_shape=(jax.ShapeDtypeStruct(block, f32),) * 2,
        in_specs=[vmem] * 4,
        out_specs=(vmem,) * 2,
        name="finish",
    )(la, lb, ra, rb)
    left_new = left_sum.reshape(64, 2, 128).transpose(1, 0, 2).reshape(2, 8192)
    right_new = right_sum.reshape(32, 4, 128).transpose(1, 0, 2).reshape(4, 4096)
    return left_new, right_new


def solution(mesh):
    in_specs = (
        P("col", "row"),
        P("row", "col"),
        P("row"),
        P(None, "row"),
        P("col"),
        P(None, "col"),
        P("row", "col"),
        P("row", "col", None),
        P("row", "col", None),
        P("row", "col", None),
    )
    out_specs = (P("col", "row"), P("row", "col"))
    return jax.shard_map(
        on_device, mesh=mesh, in_specs=in_specs, out_specs=out_specs, check_vma=False
    )
```

```python
import functools
import jax, jax.numpy as jnp
from jax import lax
from jax.sharding import PartitionSpec as P
from jax.experimental import pallas as pl
from jax.experimental.pallas import tpu as pltpu

TILE = 4096
SPT = 2048
BLOCK = 512
BLOCKS = 2 * SPT // BLOCK
PER_TILE = SPT // BLOCK
ETA = 0.5
f32, bf16, i32 = jnp.float32, jnp.bfloat16, jnp.int32


def lanes(at, size=128):
    return pl.ds(pl.multiple_of(at, 128), size)


def lane_pick(table, index):
    return jnp.take_along_axis(table, index, axis=1)


LEFT_STEPS, RIGHT_STEPS = 17, 9
PAD = 384


def upsample_matrix(up_ref):
    row = lax.broadcasted_iota(i32, (16, 128), 0)
    lane = lax.broadcasted_iota(i32, (16, 128), 1)
    for pattern in range(2):
        for offset in range(6):
            gap = (32 * pattern + 30 + offset + (lane >> 2) - row).astype(f32).astype(bf16)
            one, zero = jnp.ones((16, 128), bf16), jnp.zeros((16, 128), bf16)
            for m in range(8):
                part = jnp.where(gap == jnp.full((16, 128), 16 * m, bf16), one, zero)
                at = (pattern * 6 + offset) * 128
                up_ref[16 * m : 16 * m + 16, at : at + 128] = part
                up_ref[128 + 16 * m : 144 + 16 * m, at : at + 128] = part


def spread_weights(stencil_ref, weight_ref, by_offset_ref, origin, count):
    row = lax.broadcasted_iota(i32, (8, 128), 0)
    lane = lax.broadcasted_iota(i32, (8, 128), 1)

    def step(block, _):
        weight = jnp.concatenate(
            [weight_ref[:, lanes(block * 128)], jnp.zeros((4, 128), f32)], axis=0
        )
        stencil = jnp.broadcast_to(stencil_ref[:, lanes(block * 128)], (8, 128))
        base = stencil - (origin + block * 32) - (lane >> 2)
        by_offset_ref[:, lanes(block * 128 + PAD)] = jnp.take_along_axis(
            weight, (row - 1 - base) & 7, axis=0
        )
        return 0

    lax.fori_loop(0, count // 128, step, 0, unroll=4)


def two_terms(value):
    top = value.astype(bf16)
    return top, (value - top.astype(f32)).astype(bf16)


def coarse_windows(coarse, lhs_ref, base, steps):
    here = coarse(steps)
    for b in range(steps):
        after = coarse(b)
        mid = jnp.concatenate([here[:, 64:], after[:, :64]], axis=1)
        for w, window in enumerate((here, mid)):
            top, rest = two_terms(window)
            rows = slice(base + b * 64 + w * 32, base + b * 64 + w * 32 + 32)
            lhs_ref[rows, 0:128] = top
            lhs_ref[rows, 128:256] = rest
        here = after


def interpolate(lhs_ref, up_ref, by_offset_ref, fine_ref, base, steps):
    for tile in range(6):
        pattern, first = tile // 3, tile % 3 * 2
        got = jnp.dot(
            lhs_ref[base : base + steps * 64, :],
            up_ref[:, tile * 256 : tile * 256 + 256],
            preferred_element_type=f32,
        )
        for b in range(steps):
            for w in range(2):
                at = slice(b * 512 + (2 * w + pattern) * 128, b * 512 + (2 * w + pattern) * 128 + 128)
                weight = [
                    jnp.broadcast_to(by_offset_ref[first + n : first + n + 1, at], (8, 128))
                    for n in range(2)
                ]
                for g in range(4):
                    row = b * 64 + w * 32 + g * 8
                    part = got[row : row + 8, 0:128] * weight[0] + got[row : row + 8, 128:256] * weight[1]
                    if first:
                        part = part + fine_ref[8 * g : 8 * g + 8, at]
                    fine_ref[8 * g : 8 * g + 8, at] = part


def pick_columns(fine_ref, start, position):
    j = jnp.broadcast_to(position >> 7, (8, 128))
    lo = jnp.broadcast_to(position & 127, (8, 128))
    bits = [(j & (1 << b)) != 0 for b in range(5)]

    def tree(g, prefix, bit):
        if bit < 0:
            return lane_pick(fine_ref[8 * g : 8 * g + 8, lanes(PAD + start + prefix * 128)], lo)
        off = tree(g, prefix, bit - 1)
        on = tree(g, prefix | 1 << bit, bit - 1)
        return jnp.where(bits[bit], on, off)

    return [tree(g, 0, 4) for g in range(4)]


def build_table(fine_ref, table_ref):
    def step(hi, _):
        for h in range(2):
            j = (hi >> 1) * 4 + h * 2 + (hi & 1)
            for half in range(2):
                v = fine_ref[16 * half : 16 * half + 16, lanes(PAD + j * 128)]
                top, rest = two_terms(v)
                rows = pl.ds(pl.multiple_of(hi * 32 + 16 * half, 16), 16)
                rest_rows = pl.ds(pl.multiple_of(512 + hi * 32 + 16 * half, 16), 16)
                table_ref[rows, h * 128 : h * 128 + 128] = top
                table_ref[rest_rows, h * 128 : h * 128 + 128] = rest
        return 0

    lax.fori_loop(0, 16, step, 0, unroll=4)


def one_hot(lo):
    lo16 = jnp.broadcast_to(lo, (16, 128)) - lax.broadcasted_iota(i32, (16, 128), 0)
    lo16 = lo16.astype(f32).astype(bf16)
    one, zero = jnp.ones((16, 128), bf16), jnp.zeros((16, 128), bf16)
    return jnp.concatenate(
        [jnp.where(lo16 == jnp.full((16, 128), 16 * m, bf16), one, zero) for m in range(16)], axis=0
    )


def index_tables(position_ref, hot_ref, hi_ref, period):
    per_tile = 16 // period
    row16 = lax.broadcasted_iota(i32, (16, 128), 0)

    for tile in range(2):
        def step(n, _):
            hi, lo = split_position(position_ref[tile, :, lanes(n * 128)], period)
            at = lanes(tile * SPT + n * 128)
            hot_ref[:, at] = one_hot(lo)
            hi16 = (jnp.broadcast_to(hi, (16, 128)) - row16 // period).astype(f32).astype(bf16)
            one, zero = jnp.ones((16, 128), bf16), jnp.zeros((16, 128), bf16)
            for m in range(period):
                same = hi16 == jnp.full((16, 128), m * per_tile, bf16)
                hi_ref[16 * m : 16 * m + 16, at] = jnp.where(same, one, zero)
            return 0

        lax.fori_loop(0, SPT // 128, step, 0, unroll=2)


def table_columns(table_ref, hot, positions):
    got = jnp.dot(table_ref[...], hot, preferred_element_type=f32)
    out = []
    for sub, position in enumerate(positions):
        hi, _ = split_position(position, 4)
        hi8 = jnp.broadcast_to(hi, (8, 128))
        bits = [(hi8 & (1 << b)) != 0 for b in range(4)]

        def tree(g, prefix, bit):
            if bit < 0:
                row = prefix * 32 + 8 * g
                cut = slice(sub * 128, sub * 128 + 128)
                return got[row : row + 8, cut] + got[512 + row : 520 + row, cut]
            return jnp.where(bits[bit], tree(g, prefix | 1 << bit, bit - 1), tree(g, prefix, bit - 1))

        out.append([tree(g, 0, 3) for g in range(4)])
    return out


def sample_block(blk, fl_ref, table_ref, hot_ref, vl_ref, vr_ref, rows_ref, cols_ref, vals_ref, mask_ref):
    tile = blk // PER_TILE
    subs = [(blk % PER_TILE) * BLOCK + sub * 128 for sub in range(BLOCK // 128)]
    hot = hot_ref[:, lanes(blk * BLOCK, BLOCK)]
    rights = table_columns(table_ref, hot, [cols_ref[tile, :, lanes(at)] for at in subs])
    keep = mask_ref[0, tile].astype(f32) * -ETA
    for sub, at in enumerate(subs):
        left = pick_columns(fl_ref, tile * TILE, rows_ref[tile, :, lanes(at)])
        right = rights[sub]
        dots = (left[0] * right[0] + left[1] * right[1]) + (left[2] * right[2] + left[3] * right[3])
        error = jnp.sum(dots, axis=0, keepdims=True) - vals_ref[tile, :, lanes(at)]
        scaled = jnp.broadcast_to(error * keep, (8, 128))
        out = lanes(blk * BLOCK + sub * 128)
        for g in range(4):
            vl_ref[8 * g : 8 * g + 8, out] = scaled * right[g]
            vr_ref[8 * g : 8 * g + 8, out] = scaled * left[g]


def split_position(position, period):
    half = 8 // period
    j = position >> 7
    hi = (j // (2 * half)) * half + (j & (half - 1))
    lo = ((j // half) & 1) * 128 + (position & 127)
    return hi, lo


def scatter_block(first_sample, samples, value_ref, hot_ref, hi_ref, out_ref, period, place, at, part, parts):
    groups = range(4 * part // parts, 4 * (part + 1) // parts)
    columns = []
    for sub in range(samples // 128):
        here = lanes(first_sample + sub * 128)
        masks = [hi_ref[16 * m : 16 * m + 16, here] for m in range(period)]
        top_rows, rest_rows = [], []
        for g in groups:
            v = value_ref[8 * g : 8 * g + 8, here]
            for first in range(0, 8, period):
                index = first + lax.broadcasted_iota(i32, (8, 128), 0) % period
                dup = jnp.take_along_axis(v, index, axis=0)
                top, rest = two_terms(jnp.concatenate([dup, dup], axis=0))
                top_rows += [top * mask for mask in masks]
                rest_rows += [rest * mask for mask in masks]
        columns.append(jnp.concatenate(top_rows + rest_rows, axis=0))
    lhs = jnp.concatenate(columns, axis=1)
    rhs = hot_ref[:, lanes(first_sample, samples)]
    got = lax.dot_general(lhs, rhs, (((1,), (1,)), ((), ())), preferred_element_type=f32)
    slots = 32 // period // parts
    each = 64 * period // 32
    for slot in range(slots):
        for g in range(each):
            for h in range(2):
                row = (slot * each + g) * 8
                cut = slice(h * 128, h * 128 + 128)
                rows = pl.ds(pl.multiple_of(at + g * 16 + h * 8, 8), 8)
                both = got[row : row + 8, cut] + got[512 // parts + row : 512 // parts + row + 8, cut]
                out_ref[place(part * slots + slot), rows, :] += both


def left_place(slot):
    return slot % 2 * 8 + slot // 2 % 4 * 2 + slot // 8


def right_place(slot):
    return slot


def add_own(fine_ref, out_ref, slot, period, place):
    group = pl.multiple_of((slot * period) // 8 * 8, 8)
    row = lax.broadcasted_iota(i32, (8, 128), 0)
    index = (slot * period) % 8 + row % period
    spread = 8 // period

    def step(block, _):
        got = None
        for q in range(spread):
            tall = fine_ref[pl.ds(group, 8), lanes(PAD + (block * spread + q) * 128)]
            picked = jnp.take_along_axis(tall, index, axis=0)
            got = picked if got is None else jnp.where(row // period == q, picked, got)
        out_ref[place(slot), pl.ds(pl.multiple_of(block * 8, 8), 8), :] = got
        return 0

    lax.fori_loop(0, 16, step, 0, unroll=4)


MESH_ID = pl.DeviceIdType.MESH


def gather_coarse(r, c, cl_ref, cr_ref, gl_ref, gr_ref, edges, mains, halos):
    def send(src, dst, sems, at, to):
        return pltpu.make_async_remote_copy(
            src_ref=src, dst_ref=dst, send_sem=sems[0].at[at], recv_sem=sems[1].at[at],
            device_id=to, device_id_type=MESH_ID,
        )

    col_peers = [(d, (r, (c + d) % 16)) for d in range(1, 16)]
    row_peers = [(15 + d, ((r + d) % 8, c)) for d in range(1, 8)]
    left_edges = [
        send(cl_ref.at[:, 0:128], gl_ref.at[c, :, 2048:2176], edges, 0, ((r + 7) % 8, c)),
        send(cl_ref.at[:, 1920:2048], gl_ref.at[c, :, 2176:2304], edges, 1, ((r + 1) % 8, c)),
    ]
    right_edges = [
        send(cr_ref.at[:, 0:128], gr_ref.at[r, :, 1024:1152], edges, 2, (r, (c + 15) % 16)),
        send(cr_ref.at[:, 896:1024], gr_ref.at[r, :, 1152:1280], edges, 3, (r, (c + 1) % 16)),
    ]
    left_mains = [send(cl_ref, gl_ref.at[c, :, 0:2048], mains, at, to) for at, to in col_peers]
    right_mains = [send(cr_ref, gr_ref.at[r, :, 0:1024], mains, at, to) for at, to in row_peers]
    own_left, own_right = gl_ref.at[c, :, 2048:2304], gr_ref.at[r, :, 1024:1280]
    left_halos = [send(own_left, own_left, halos, at, to) for at, to in col_peers]
    right_halos = [send(own_right, own_right, halos, at, to) for at, to in row_peers]

    def begin():
        for copy in left_edges + right_edges + right_mains + left_mains:
            copy.start()
        gl_ref[c, :, 0:2048] = cl_ref[...]
        gr_ref[r, :, 0:1024] = cr_ref[...]

    def forward():
        for copy in right_edges:
            copy.wait()
        for copy in right_halos:
            copy.start()
        for copy in left_edges:
            copy.wait()
        for copy in left_halos:
            copy.start()

    def end_right():
        for copy in right_mains + right_halos:
            copy.wait()

        @pl.when(c == 0)
        def _():
            gr_ref[:, :, 1152:1280] = jnp.zeros((8, 4, 128), f32)

        @pl.when(c == 15)
        def _():
            gr_ref[:, :, 1024:1152] = jnp.zeros((8, 4, 128), f32)

    def end_left():
        for copy in left_mains + left_halos:
            copy.wait()

        @pl.when(r == 0)
        def _():
            gl_ref[:, :, 2176:2304] = jnp.zeros((16, 2, 128), f32)

        @pl.when(r == 7)
        def _():
            gl_ref[:, :, 2048:2176] = jnp.zeros((16, 2, 128), f32)

    return begin, forward, end_right, end_left


class Exchange:
    def __init__(self, r, c, pl_ref, pr_ref, la_ref, lb_ref, ra_ref, rb_ref, work, sends, recvs, out_sem):
        self.pair_ref, self.sum_ref, self.ly_ref, self.lsum_ref, self.rx_ref, self.rsum_ref = work
        self.pl_ref, self.pr_ref = pl_ref, pr_ref
        self.la_ref, self.lb_ref, self.ra_ref, self.rb_ref = la_ref, lb_ref, ra_ref, rb_ref
        self.sends, self.recvs, self.out_sem = sends, recvs, out_sem
        self.zlo, self.x = r // 4, r % 4
        self.zhi, self.y, self.core = c // 8, (c // 2) % 4, c % 2
        self.r, self.c = r, c

    def send(self, src, dst, at, to):
        return pltpu.make_async_remote_copy(
            src_ref=src, dst_ref=dst, send_sem=self.sends.at[at], recv_sem=self.recvs.at[at],
            device_id=to, device_id_type=MESH_ID,
        )

    def pair(self, p):
        cut = pl.ds(p * 64, 64)
        return self.send(
            self.pl_ref.at[pl.ds((1 - self.core) * 8, 8), cut], self.pair_ref.at[:, cut], p,
            (self.r, self.c + 1 - 2 * self.core),
        )

    def along_y(self, p):
        cut = pl.ds(p * 64, 64)
        out = []
        for d in range(1, 4):
            there = (self.y + d) % 4
            out.append(self.send(
                self.sum_ref.at[pl.ds(there * 2, 2), cut], self.ly_ref.at[d - 1, :, cut],
                2 + p * 3 + d - 1, (self.r, self.zhi * 8 + there * 2 + self.core),
            ))
        return out

    def left_z(self, p):
        cut = pl.ds(p * 64, 64)
        return self.send(
            self.lsum_ref.at[1 - self.zhi, cut], self.lb_ref.at[cut], 8 + p, (self.r, (self.c + 8) % 16)
        )

    def along_x(self, half):
        out = []
        for d in range(1, 4):
            there = (self.x + d) % 4
            out.append(self.send(
                self.pr_ref.at[half * 4 + there], self.rx_ref.at[half, d - 1],
                10 + half * 3 + d - 1, (self.zlo * 4 + there, self.c),
            ))
        return out

    def right_z(self):
        return self.send(
            self.rsum_ref.at[1 - self.zlo], self.rb_ref, 16, ((self.r + 4) % 8, self.c)
        )

    def after_pair(self, p):
        cut = pl.ds(p * 64, 64)
        self.pair(p).wait()
        for s in range(8):
            self.sum_ref[s, cut] = self.pl_ref[self.core * 8 + s, cut] + self.pair_ref[s, cut]
        for copy in self.along_y(p):
            copy.start()

    def after_y(self, p):
        cut = pl.ds(p * 64, 64)
        for copy in self.along_y(p):
            copy.wait()
        for s in range(2):
            self.lsum_ref[s, cut] = self.sum_ref[self.y * 2 + s, cut] + (
                self.ly_ref[0, s, cut] + self.ly_ref[1, s, cut] + self.ly_ref[2, s, cut]
            )
        self.left_z(p).start()

    def after_x(self, half):
        for copy in self.along_x(half):
            copy.wait()
        self.rsum_ref[half] = self.pr_ref[half * 4 + self.x] + (
            self.rx_ref[half, 0] + self.rx_ref[half, 1] + self.rx_ref[half, 2]
        )

        @pl.when(self.zlo == 1 - half)
        def _():
            self.right_z().start()

    def own(self):
        return (
            pltpu.make_async_copy(self.lsum_ref.at[self.zhi], self.la_ref, self.out_sem.at[0]),
            pltpu.make_async_copy(self.rsum_ref.at[self.zlo], self.ra_ref, self.out_sem.at[1]),
        )

    def end(self):
        for copy in self.own():
            copy.start()
        self.left_z(0).wait()
        self.left_z(1).wait()
        self.right_z().wait()
        for copy in self.own():
            copy.wait()


def step_kernel(
    mask_in, cl_in, cr_in, sl_in, wl_in, sr_in, wr_in, rows_in, cols_in, vals_in,
    la_ref, lb_ref, ra_ref, rb_ref,
    mask_ref, cl_ref, cr_ref, sl_ref, wl_ref, sr_ref, wr_ref, rows_ref, cols_ref, vals_ref, in_sem, out_sem,
    gl_ref, gr_ref, fl_ref, fr_ref, wl6_ref, wr6_ref, vl_ref, vr_ref, pl_ref, pr_ref,
    pair_ref, sum_ref, ly_ref, lsum_ref, rx_ref, rsum_ref,
    edge_send, edge_recv, main_send, main_recv, halo_send, halo_recv, sends, recvs,
):
    r = lax.axis_index("row")
    c = lax.axis_index("col")
    peers = [(r, (c + d) % 16) for d in range(1, 16)] + [((r + d) % 8, c) for d in range(1, 8)]
    barrier = pltpu.get_barrier_semaphore()
    for peer in peers:
        pl.semaphore_signal(barrier, inc=1, device_id=peer, device_id_type=MESH_ID)
    pairs = (
        (sr_in, sr_ref), (wr_in, wr_ref), (sl_in, sl_ref), (wl_in, wl_ref), (cl_in, cl_ref), (cr_in, cr_ref),
        (cols_in, cols_ref), (rows_in, rows_ref), (vals_in, vals_ref), (mask_in, mask_ref),
    )
    loads = [pltpu.make_async_copy(src, dst, in_sem.at[n]) for n, (src, dst) in enumerate(pairs)]
    for load in loads:
        load.start()
    begin, forward, end_right, end_left = gather_coarse(
        r, c, cl_ref, cr_ref, gl_ref, gr_ref,
        (edge_send, edge_recv), (main_send, main_recv), (halo_send, halo_recv),
    )
    exchange = Exchange(
        r, c, pl_ref, pr_ref, la_ref, lb_ref, ra_ref, rb_ref,
        (pair_ref, sum_ref, ly_ref, lsum_ref, rx_ref, rsum_ref), sends, recvs, out_sem,
    )

    def local(up_ref, lhs_ref, table_ref, hotr_ref, hotc_ref, hir_ref, hic_ref):
        upsample_matrix(up_ref)
        for load in loads:
            load.wait()
        spread_weights(sr_ref, wr_ref, wr6_ref, c * 1024, 4096)
        spread_weights(sl_ref, wl_ref, wl6_ref, r * 2048, 8192)
        pl.semaphore_wait(barrier, len(peers))
        begin()
        index_tables(cols_ref, hotc_ref, hic_ref, 4)
        forward()
        index_tables(rows_ref, hotr_ref, hir_ref, 2)
        pl_ref[...] = jnp.zeros(pl_ref.shape, f32)
        pr_ref[...] = jnp.zeros(pr_ref.shape, f32)
        end_right()
        right_base = LEFT_STEPS * 64
        coarse_windows(
            lambda b: gr_ref[:, :, lanes(b * 128)].reshape(32, 128), lhs_ref, right_base, RIGHT_STEPS
        )
        interpolate(lhs_ref, up_ref, wr6_ref, fr_ref, right_base, RIGHT_STEPS)
        build_table(fr_ref, table_ref)
        add_own(fr_ref, pr_ref, r, 4, right_place)
        end_left()
        coarse_windows(lambda b: gl_ref[:, :, lanes(b * 128)].reshape(32, 128), lhs_ref, 0, LEFT_STEPS)
        interpolate(lhs_ref, up_ref, wl6_ref, fl_ref, 0, LEFT_STEPS)
        add_own(fl_ref, pl_ref, c, 2, left_place)

        def sample(blk):
            sample_block(
                blk, fl_ref, table_ref, hotc_ref, vl_ref, vr_ref, rows_ref, cols_ref, vals_ref, mask_ref
            )

        def scatter(blk):
            at = blk // PER_TILE * 64
            scatter_block(
                blk * BLOCK, BLOCK, vl_ref, hotr_ref, hir_ref, pl_ref, 2, left_place, at, 0, 1
            )
            scatter_block(
                blk * BLOCK, BLOCK, vr_ref, hotc_ref, hic_ref, pr_ref, 4, right_place, 0, 0, 2
            )

        sample(0)

        @pl.loop(1, BLOCKS)
        def _(blk):
            scatter(blk - 1)
            sample(blk)

            @pl.when(blk == PER_TILE)
            def _():
                exchange.pair(0).start()

            @pl.when(blk == PER_TILE + 2)
            def _():
                exchange.after_pair(0)

        scatter(BLOCKS - 1)
        exchange.pair(1).start()
        for copy in exchange.along_x(0):
            copy.start()

        @pl.loop(0, BLOCKS // 2)
        def _(step):
            scatter_block(
                step * 2 * BLOCK, 2 * BLOCK, vr_ref, hotc_ref, hic_ref, pr_ref, 4, right_place, 0, 1, 2
            )

            @pl.when(step == BLOCKS // 2 - 2)
            def _():
                exchange.after_pair(1)

        for copy in exchange.along_x(1):
            copy.start()
        exchange.after_y(0)
        exchange.after_x(0)
        exchange.after_y(1)
        exchange.after_x(1)
        exchange.end()

    pl.run_scoped(
        local,
        pltpu.VMEM((256, 1536), bf16),
        pltpu.VMEM(((LEFT_STEPS + RIGHT_STEPS) * 64, 256), bf16),
        pltpu.VMEM((1024, 256), bf16),
        pltpu.VMEM((256, 2 * SPT), bf16),
        pltpu.VMEM((256, 2 * SPT), bf16),
        pltpu.VMEM((32, 2 * SPT), bf16),
        pltpu.VMEM((64, 2 * SPT), bf16),
    )


def finish_kernel(la_ref, lb_ref, ra_ref, rb_ref, left_ref, right_ref):
    left_ref[...] = la_ref[...] + lb_ref[...]
    right_ref[...] = ra_ref[...] + rb_ref[...]


def on_device(coarse_left, coarse_right, sl, wl, sr, wr, mask, rows, cols, vals):
    vmem = pl.BlockSpec(memory_space=pltpu.VMEM)
    anywhere = pl.BlockSpec(memory_space=pl.ANY)
    operands = (
        mask.reshape(1, 2), coarse_left, coarse_right, sl.reshape(1, -1), wl, sr.reshape(1, -1), wr,
        rows, cols, vals,
    )
    dma = pltpu.SemaphoreType.DMA
    block = (128, 128)
    la, lb, ra, rb = pl.pallas_call(
        step_kernel,
        out_shape=(jax.ShapeDtypeStruct(block, f32),) * 4,
        in_specs=[anywhere] * 10,
        out_specs=(anywhere,) * 4,
        scratch_shapes=[
            pltpu.SMEM((1, 2), i32),
            *[pltpu.VMEM(a.shape, a.dtype) for a in operands[1:]],
            dma((10,)),
            dma((2,)),
            pltpu.VMEM((16, 2, 2304), f32),
            pltpu.VMEM((8, 4, 1280), f32),
            pltpu.VMEM((32, 512 * LEFT_STEPS), f32),
            pltpu.VMEM((32, 512 * RIGHT_STEPS), f32),
            pltpu.VMEM((8, 512 * LEFT_STEPS), f32),
            pltpu.VMEM((8, 512 * RIGHT_STEPS), f32),
            pltpu.VMEM((32, 2 * SPT), f32),
            pltpu.VMEM((32, 2 * SPT), f32),
            pltpu.VMEM((16, *block), f32),
            pltpu.VMEM((8, *block), f32),
            pltpu.VMEM((8, *block), f32),
            pltpu.VMEM((8, *block), f32),
            pltpu.VMEM((3, 2, *block), f32),
            pltpu.VMEM((2, *block), f32),
            pltpu.VMEM((2, 3, *block), f32),
            pltpu.VMEM((2, *block), f32),
            dma((4,)), dma((4,)), dma((23,)), dma((23,)), dma((23,)), dma((23,)),
            dma((17,)), dma((17,)),
        ],
        compiler_params=pltpu.CompilerParams(collective_id=0, has_side_effects=True),
        name="fused_step",
    )(*operands)
    left_sum, right_sum = pl.pallas_call(
        finish_kernel,
        out_shape=(jax.ShapeDtypeStruct(block, f32),) * 2,
        in_specs=[vmem] * 4,
        out_specs=(vmem,) * 2,
        name="finish",
    )(la, lb, ra, rb)
    left_new = left_sum.reshape(64, 2, 128).transpose(1, 0, 2).reshape(2, 8192)
    right_new = right_sum.reshape(32, 4, 128).transpose(1, 0, 2).reshape(4, 4096)
    return left_new, right_new


def solution(mesh):
    in_specs = (
        P("col", "row"),
        P("row", "col"),
        P("row"),
        P(None, "row"),
        P("col"),
        P(None, "col"),
        P("row", "col"),
        P("row", "col", None),
        P("row", "col", None),
        P("row", "col", None),
    )
    out_specs = (P("col", "row"), P("row", "col"))
    return jax.shard_map(
        on_device, mesh=mesh, in_specs=in_specs, out_specs=out_specs, check_vma=False
    )
```

```python
import functools
import jax, jax.numpy as jnp
from jax import lax
from jax.sharding import PartitionSpec as P
from jax.experimental import pallas as pl
from jax.experimental.pallas import tpu as pltpu

TILE = 4096
SPT = 2048
BLOCK = 512
BLOCKS = 2 * SPT // BLOCK
PER_TILE = SPT // BLOCK
ETA = 0.5
f32, bf16, i32 = jnp.float32, jnp.bfloat16, jnp.int32


def lanes(at, size=128):
    return pl.ds(pl.multiple_of(at, 128), size)


def lane_pick(table, index):
    return jnp.take_along_axis(table, index, axis=1)


LEFT_STEPS, RIGHT_STEPS = 17, 9
PAD = 384


def upsample_matrix(up_ref):
    row = lax.broadcasted_iota(i32, (16, 128), 0)
    lane = lax.broadcasted_iota(i32, (16, 128), 1)
    for pattern in range(2):
        for offset in range(6):
            gap = (32 * pattern + 30 + offset + (lane >> 2) - row).astype(f32).astype(bf16)
            one, zero = jnp.ones((16, 128), bf16), jnp.zeros((16, 128), bf16)
            for m in range(8):
                part = jnp.where(gap == jnp.full((16, 128), 16 * m, bf16), one, zero)
                at = (pattern * 6 + offset) * 128
                up_ref[16 * m : 16 * m + 16, at : at + 128] = part
                up_ref[128 + 16 * m : 144 + 16 * m, at : at + 128] = part


def spread_weights(stencil_ref, weight_ref, by_offset_ref, origin, count):
    row = lax.broadcasted_iota(i32, (8, 128), 0)
    lane = lax.broadcasted_iota(i32, (8, 128), 1)

    def step(block, _):
        weight = jnp.concatenate(
            [weight_ref[:, lanes(block * 128)], jnp.zeros((4, 128), f32)], axis=0
        )
        stencil = jnp.broadcast_to(stencil_ref[:, lanes(block * 128)], (8, 128))
        base = stencil - (origin + block * 32) - (lane >> 2)
        by_offset_ref[:, lanes(block * 128 + PAD)] = jnp.take_along_axis(
            weight, (row - 1 - base) & 7, axis=0
        )
        return 0

    lax.fori_loop(0, count // 128, step, 0, unroll=4)


def two_terms(value):
    top = value.astype(bf16)
    return top, (value - top.astype(f32)).astype(bf16)


def coarse_windows(coarse, lhs_ref, base, steps):
    here = coarse(steps)
    for b in range(steps):
        after = coarse(b)
        mid = jnp.concatenate([here[:, 64:], after[:, :64]], axis=1)
        for w, window in enumerate((here, mid)):
            top, rest = two_terms(window)
            rows = slice(base + b * 64 + w * 32, base + b * 64 + w * 32 + 32)
            lhs_ref[rows, 0:128] = top
            lhs_ref[rows, 128:256] = rest
        here = after


def interpolate(lhs_ref, up_ref, by_offset_ref, fine_ref, base, steps):
    for tile in range(6):
        pattern, first = tile // 3, tile % 3 * 2
        got = jnp.dot(
            lhs_ref[base : base + steps * 64, :],
            up_ref[:, tile * 256 : tile * 256 + 256],
            preferred_element_type=f32,
        )
        for b in range(steps):
            for w in range(2):
                at = slice(b * 512 + (2 * w + pattern) * 128, b * 512 + (2 * w + pattern) * 128 + 128)
                weight = [
                    jnp.broadcast_to(by_offset_ref[first + n : first + n + 1, at], (8, 128))
                    for n in range(2)
                ]
                for g in range(4):
                    row = b * 64 + w * 32 + g * 8
                    part = got[row : row + 8, 0:128] * weight[0] + got[row : row + 8, 128:256] * weight[1]
                    if first:
                        part = part + fine_ref[8 * g : 8 * g + 8, at]
                    fine_ref[8 * g : 8 * g + 8, at] = part


def pick_columns(fine_ref, start, position):
    j = jnp.broadcast_to(position >> 7, (8, 128))
    lo = jnp.broadcast_to(position & 127, (8, 128))
    bits = [(j & (1 << b)) != 0 for b in range(5)]

    def tree(g, prefix, bit):
        if bit < 0:
            return lane_pick(fine_ref[8 * g : 8 * g + 8, lanes(PAD + start + prefix * 128)], lo)
        off = tree(g, prefix, bit - 1)
        on = tree(g, prefix | 1 << bit, bit - 1)
        return jnp.where(bits[bit], on, off)

    return [tree(g, 0, 4) for g in range(4)]


def build_table(fine_ref, table_ref):
    def step(hi, _):
        for h in range(2):
            j = (hi >> 1) * 4 + h * 2 + (hi & 1)
            for half in range(2):
                v = fine_ref[16 * half : 16 * half + 16, lanes(PAD + j * 128)]
                top, rest = two_terms(v)
                rows = pl.ds(pl.multiple_of(hi * 32 + 16 * half, 16), 16)
                rest_rows = pl.ds(pl.multiple_of(512 + hi * 32 + 16 * half, 16), 16)
                table_ref[rows, h * 128 : h * 128 + 128] = top
                table_ref[rest_rows, h * 128 : h * 128 + 128] = rest
        return 0

    lax.fori_loop(0, 16, step, 0, unroll=4)


def one_hot(lo):
    lo16 = jnp.broadcast_to(lo, (16, 128)) - lax.broadcasted_iota(i32, (16, 128), 0)
    lo16 = lo16.astype(f32).astype(bf16)
    one, zero = jnp.ones((16, 128), bf16), jnp.zeros((16, 128), bf16)
    return jnp.concatenate(
        [jnp.where(lo16 == jnp.full((16, 128), 16 * m, bf16), one, zero) for m in range(16)], axis=0
    )


def index_tables(position_ref, hot_ref, hi_ref, period):
    per_tile = 16 // period
    row16 = lax.broadcasted_iota(i32, (16, 128), 0)

    for tile in range(2):
        def step(n, _):
            hi, lo = split_position(position_ref[tile, :, lanes(n * 128)], period)
            at = lanes(tile * SPT + n * 128)
            hot_ref[:, at] = one_hot(lo)
            hi16 = (jnp.broadcast_to(hi, (16, 128)) - row16 // period).astype(f32).astype(bf16)
            one, zero = jnp.ones((16, 128), bf16), jnp.zeros((16, 128), bf16)
            for m in range(period):
                same = hi16 == jnp.full((16, 128), m * per_tile, bf16)
                hi_ref[16 * m : 16 * m + 16, at] = jnp.where(same, one, zero)
            return 0

        lax.fori_loop(0, SPT // 128, step, 0, unroll=2)


def table_columns(table_ref, hot, positions):
    got = jnp.dot(table_ref[...], hot, preferred_element_type=f32)
    out = []
    for sub, position in enumerate(positions):
        hi, _ = split_position(position, 4)
        hi8 = jnp.broadcast_to(hi, (8, 128))
        bits = [(hi8 & (1 << b)) != 0 for b in range(4)]

        def tree(g, prefix, bit):
            if bit < 0:
                row = prefix * 32 + 8 * g
                cut = slice(sub * 128, sub * 128 + 128)
                return got[row : row + 8, cut] + got[512 + row : 520 + row, cut]
            return jnp.where(bits[bit], tree(g, prefix | 1 << bit, bit - 1), tree(g, prefix, bit - 1))

        out.append([tree(g, 0, 3) for g in range(4)])
    return out


def sample_block(blk, fl_ref, table_ref, hot_ref, vl_ref, vr_ref, rows_ref, cols_ref, vals_ref, mask_ref):
    tile = blk // PER_TILE
    subs = [(blk % PER_TILE) * BLOCK + sub * 128 for sub in range(BLOCK // 128)]
    hot = hot_ref[:, lanes(blk * BLOCK, BLOCK)]
    rights = table_columns(table_ref, hot, [cols_ref[tile, :, lanes(at)] for at in subs])
    keep = mask_ref[0, tile].astype(f32) * -ETA
    for sub, at in enumerate(subs):
        left = pick_columns(fl_ref, tile * TILE, rows_ref[tile, :, lanes(at)])
        right = rights[sub]
        dots = (left[0] * right[0] + left[1] * right[1]) + (left[2] * right[2] + left[3] * right[3])
        error = jnp.sum(dots, axis=0, keepdims=True) - vals_ref[tile, :, lanes(at)]
        scaled = jnp.broadcast_to(error * keep, (8, 128))
        out = lanes(blk * BLOCK + sub * 128)
        for g in range(4):
            vl_ref[8 * g : 8 * g + 8, out] = scaled * right[g]
            vr_ref[8 * g : 8 * g + 8, out] = scaled * left[g]


def split_position(position, period):
    half = 8 // period
    j = position >> 7
    hi = (j // (2 * half)) * half + (j & (half - 1))
    lo = ((j // half) & 1) * 128 + (position & 127)
    return hi, lo


def scatter_block(first_sample, samples, value_ref, hot_ref, hi_ref, out_ref, period, place, at, part, parts):
    groups = range(4 * part // parts, 4 * (part + 1) // parts)
    columns = []
    for sub in range(samples // 128):
        here = lanes(first_sample + sub * 128)
        masks = [hi_ref[16 * m : 16 * m + 16, here] for m in range(period)]
        top_rows, rest_rows = [], []
        for g in groups:
            v = value_ref[8 * g : 8 * g + 8, here]
            for first in range(0, 8, period):
                index = first + lax.broadcasted_iota(i32, (8, 128), 0) % period
                dup = jnp.take_along_axis(v, index, axis=0)
                top, rest = two_terms(jnp.concatenate([dup, dup], axis=0))
                top_rows += [top * mask for mask in masks]
                rest_rows += [rest * mask for mask in masks]
        columns.append(jnp.concatenate(top_rows + rest_rows, axis=0))
    lhs = jnp.concatenate(columns, axis=1)
    rhs = hot_ref[:, lanes(first_sample, samples)]
    got = lax.dot_general(lhs, rhs, (((1,), (1,)), ((), ())), preferred_element_type=f32)
    slots = 32 // period // parts
    each = 64 * period // 32
    for slot in range(slots):
        for g in range(each):
            for h in range(2):
                row = (slot * each + g) * 8
                cut = slice(h * 128, h * 128 + 128)
                rows = pl.ds(pl.multiple_of(at + g * 16 + h * 8, 8), 8)
                both = got[row : row + 8, cut] + got[512 // parts + row : 512 // parts + row + 8, cut]
                out_ref[place(part * slots + slot), rows, :] += both


def left_place(slot):
    return slot % 2 * 8 + slot // 2 % 4 * 2 + slot // 8


def right_place(slot):
    return slot


def add_own(fine_ref, out_ref, slot, period, place):
    group = pl.multiple_of((slot * period) // 8 * 8, 8)
    row = lax.broadcasted_iota(i32, (8, 128), 0)
    index = (slot * period) % 8 + row % period
    spread = 8 // period

    def step(block, _):
        got = None
        for q in range(spread):
            tall = fine_ref[pl.ds(group, 8), lanes(PAD + (block * spread + q) * 128)]
            picked = jnp.take_along_axis(tall, index, axis=0)
            got = picked if got is None else jnp.where(row // period == q, picked, got)
        out_ref[place(slot), pl.ds(pl.multiple_of(block * 8, 8), 8), :] = got
        return 0

    lax.fori_loop(0, 16, step, 0, unroll=4)


MESH_ID = pl.DeviceIdType.MESH


def gather_coarse(r, c, cl_ref, cr_ref, gl_ref, gr_ref, edges, mains, halos):
    def send(src, dst, sems, at, to):
        return pltpu.make_async_remote_copy(
            src_ref=src, dst_ref=dst, send_sem=sems[0].at[at], recv_sem=sems[1].at[at],
            device_id=to, device_id_type=MESH_ID,
        )

    col_peers = [(d, (r, (c + d) % 16)) for d in range(1, 16)]
    row_peers = [(15 + d, ((r + d) % 8, c)) for d in range(1, 8)]
    left_edges = [
        send(cl_ref.at[:, 0:128], gl_ref.at[c, :, 2048:2176], edges, 0, ((r + 7) % 8, c)),
        send(cl_ref.at[:, 1920:2048], gl_ref.at[c, :, 2176:2304], edges, 1, ((r + 1) % 8, c)),
    ]
    right_edges = [
        send(cr_ref.at[:, 0:128], gr_ref.at[r, :, 1024:1152], edges, 2, (r, (c + 15) % 16)),
        send(cr_ref.at[:, 896:1024], gr_ref.at[r, :, 1152:1280], edges, 3, (r, (c + 1) % 16)),
    ]
    left_mains = [send(cl_ref, gl_ref.at[c, :, 0:2048], mains, at, to) for at, to in col_peers]
    right_mains = [send(cr_ref, gr_ref.at[r, :, 0:1024], mains, at, to) for at, to in row_peers]
    own_left, own_right = gl_ref.at[c, :, 2048:2304], gr_ref.at[r, :, 1024:1280]
    left_halos = [send(own_left, own_left, halos, at, to) for at, to in col_peers]
    right_halos = [send(own_right, own_right, halos, at, to) for at, to in row_peers]

    def begin():
        for copy in left_edges + right_edges + right_mains + left_mains:
            copy.start()
        gl_ref[c, :, 0:2048] = cl_ref[...]
        gr_ref[r, :, 0:1024] = cr_ref[...]

    def forward():
        for copy in right_edges:
            copy.wait()
        for copy in right_halos:
            copy.start()
        for copy in left_edges:
            copy.wait()
        for copy in left_halos:
            copy.start()

    def end_right():
        for copy in right_mains + right_halos:
            copy.wait()

        @pl.when(c == 0)
        def _():
            gr_ref[:, :, 1152:1280] = jnp.zeros((8, 4, 128), f32)

        @pl.when(c == 15)
        def _():
            gr_ref[:, :, 1024:1152] = jnp.zeros((8, 4, 128), f32)

    def end_left():
        for copy in left_mains + left_halos:
            copy.wait()

        @pl.when(r == 0)
        def _():
            gl_ref[:, :, 2176:2304] = jnp.zeros((16, 2, 128), f32)

        @pl.when(r == 7)
        def _():
            gl_ref[:, :, 2048:2176] = jnp.zeros((16, 2, 128), f32)

    return begin, forward, end_right, end_left


class Exchange:
    def __init__(self, r, c, pl_ref, pr_ref, la_ref, lb_ref, ra_ref, rb_ref, work, sends, recvs, out_sem):
        self.pair_ref, self.sum_ref, self.ly_ref, self.lsum_ref, self.rx_ref, self.rsum_ref = work
        self.pl_ref, self.pr_ref = pl_ref, pr_ref
        self.la_ref, self.lb_ref, self.ra_ref, self.rb_ref = la_ref, lb_ref, ra_ref, rb_ref
        self.sends, self.recvs, self.out_sem = sends, recvs, out_sem
        self.zlo, self.x = r // 4, r % 4
        self.zhi, self.y, self.core = c // 8, (c // 2) % 4, c % 2
        self.r, self.c = r, c

    def send(self, src, dst, at, to):
        return pltpu.make_async_remote_copy(
            src_ref=src, dst_ref=dst, send_sem=self.sends.at[at], recv_sem=self.recvs.at[at],
            device_id=to, device_id_type=MESH_ID,
        )

    def pair(self, p):
        cut = pl.ds(p * 64, 64)
        return self.send(
            self.pl_ref.at[pl.ds((1 - self.core) * 8, 8), cut], self.pair_ref.at[:, cut], p,
            (self.r, self.c + 1 - 2 * self.core),
        )

    def along_y(self, p):
        cut = pl.ds(p * 64, 64)
        out = []
        for d in range(1, 4):
            there = (self.y + d) % 4
            out.append(self.send(
                self.sum_ref.at[pl.ds(there * 2, 2), cut], self.ly_ref.at[d - 1, :, cut],
                2 + p * 3 + d - 1, (self.r, self.zhi * 8 + there * 2 + self.core),
            ))
        return out

    def left_z(self, p):
        cut = pl.ds(p * 64, 64)
        return self.send(
            self.lsum_ref.at[1 - self.zhi, cut], self.lb_ref.at[cut], 8 + p, (self.r, (self.c + 8) % 16)
        )

    def along_x(self, half):
        out = []
        for d in range(1, 4):
            there = (self.x + d) % 4
            out.append(self.send(
                self.pr_ref.at[half * 4 + there], self.rx_ref.at[half, d - 1],
                10 + half * 3 + d - 1, (self.zlo * 4 + there, self.c),
            ))
        return out

    def right_z(self):
        return self.send(
            self.rsum_ref.at[1 - self.zlo], self.rb_ref, 16, ((self.r + 4) % 8, self.c)
        )

    def after_pair(self, p):
        cut = pl.ds(p * 64, 64)
        self.pair(p).wait()
        for s in range(8):
            self.sum_ref[s, cut] = self.pl_ref[self.core * 8 + s, cut] + self.pair_ref[s, cut]
        for copy in self.along_y(p):
            copy.start()

    def after_y(self, p):
        cut = pl.ds(p * 64, 64)
        for copy in self.along_y(p):
            copy.wait()
        for s in range(2):
            self.lsum_ref[s, cut] = self.sum_ref[self.y * 2 + s, cut] + (
                self.ly_ref[0, s, cut] + self.ly_ref[1, s, cut] + self.ly_ref[2, s, cut]
            )
        self.left_z(p).start()

    def after_x(self, half):
        for copy in self.along_x(half):
            copy.wait()
        self.rsum_ref[half] = self.pr_ref[half * 4 + self.x] + (
            self.rx_ref[half, 0] + self.rx_ref[half, 1] + self.rx_ref[half, 2]
        )

        @pl.when(self.zlo == 1 - half)
        def _():
            self.right_z().start()

    def own(self):
        return (
            pltpu.make_async_copy(self.lsum_ref.at[self.zhi], self.la_ref, self.out_sem.at[0]),
            pltpu.make_async_copy(self.rsum_ref.at[self.zlo], self.ra_ref, self.out_sem.at[1]),
        )

    def end(self):
        for copy in self.own():
            copy.start()
        self.left_z(0).wait()
        self.left_z(1).wait()
        self.right_z().wait()
        for copy in self.own():
            copy.wait()


def step_kernel(
    mask_in, cl_in, cr_in, sl_in, wl_in, sr_in, wr_in, rows_in, cols_in, vals_in,
    la_ref, lb_ref, ra_ref, rb_ref,
    mask_ref, cl_ref, cr_ref, sl_ref, wl_ref, sr_ref, wr_ref, rows_ref, cols_ref, vals_ref, in_sem, out_sem,
    gl_ref, gr_ref, fl_ref, fr_ref, wl6_ref, wr6_ref, vl_ref, vr_ref, pl_ref, pr_ref,
    pair_ref, sum_ref, ly_ref, lsum_ref, rx_ref, rsum_ref,
    edge_send, edge_recv, main_send, main_recv, halo_send, halo_recv, sends, recvs,
):
    r = lax.axis_index("row")
    c = lax.axis_index("col")
    peers = [(r, (c + d) % 16) for d in range(1, 16)] + [((r + d) % 8, c) for d in range(1, 8)]
    barrier = pltpu.get_barrier_semaphore()
    for peer in peers:
        pl.semaphore_signal(barrier, inc=1, device_id=peer, device_id_type=MESH_ID)
    pairs = (
        (sr_in, sr_ref), (wr_in, wr_ref), (sl_in, sl_ref), (wl_in, wl_ref), (cl_in, cl_ref), (cr_in, cr_ref),
        (cols_in, cols_ref), (rows_in, rows_ref), (vals_in, vals_ref), (mask_in, mask_ref),
    )
    loads = [pltpu.make_async_copy(src, dst, in_sem.at[n]) for n, (src, dst) in enumerate(pairs)]
    for load in loads:
        load.start()
    begin, forward, end_right, end_left = gather_coarse(
        r, c, cl_ref, cr_ref, gl_ref, gr_ref,
        (edge_send, edge_recv), (main_send, main_recv), (halo_send, halo_recv),
    )
    exchange = Exchange(
        r, c, pl_ref, pr_ref, la_ref, lb_ref, ra_ref, rb_ref,
        (pair_ref, sum_ref, ly_ref, lsum_ref, rx_ref, rsum_ref), sends, recvs, out_sem,
    )

    def local(up_ref, lhs_ref, table_ref, hotr_ref, hotc_ref, hir_ref, hic_ref):
        upsample_matrix(up_ref)
        for load in loads:
            load.wait()
        spread_weights(sr_ref, wr_ref, wr6_ref, c * 1024, 4096)
        spread_weights(sl_ref, wl_ref, wl6_ref, r * 2048, 8192)
        pl.semaphore_wait(barrier, len(peers))
        begin()
        index_tables(cols_ref, hotc_ref, hic_ref, 4)
        forward()
        index_tables(rows_ref, hotr_ref, hir_ref, 2)
        pl_ref[...] = jnp.zeros(pl_ref.shape, f32)
        pr_ref[...] = jnp.zeros(pr_ref.shape, f32)
        end_right()
        right_base = LEFT_STEPS * 64
        coarse_windows(
            lambda b: gr_ref[:, :, lanes(b * 128)].reshape(32, 128), lhs_ref, right_base, RIGHT_STEPS
        )
        interpolate(lhs_ref, up_ref, wr6_ref, fr_ref, right_base, RIGHT_STEPS)
        build_table(fr_ref, table_ref)
        add_own(fr_ref, pr_ref, r, 4, right_place)
        end_left()
        coarse_windows(lambda b: gl_ref[:, :, lanes(b * 128)].reshape(32, 128), lhs_ref, 0, LEFT_STEPS)
        interpolate(lhs_ref, up_ref, wl6_ref, fl_ref, 0, LEFT_STEPS)
        add_own(fl_ref, pl_ref, c, 2, left_place)

        def sample(blk):
            sample_block(
                blk, fl_ref, table_ref, hotc_ref, vl_ref, vr_ref, rows_ref, cols_ref, vals_ref, mask_ref
            )

        def scatter(blk):
            at = blk // PER_TILE * 64
            scatter_block(
                blk * BLOCK, BLOCK, vl_ref, hotr_ref, hir_ref, pl_ref, 2, left_place, at, 0, 1
            )
            scatter_block(
                blk * BLOCK, BLOCK, vr_ref, hotc_ref, hic_ref, pr_ref, 4, right_place, 0, 0, 2
            )

        sample(0)

        @pl.loop(1, BLOCKS)
        def _(blk):
            scatter(blk - 1)
            sample(blk)

            @pl.when(blk == PER_TILE)
            def _():
                exchange.pair(0).start()

            @pl.when(blk == PER_TILE + 1)
            def _():
                exchange.after_pair(0)

        scatter(BLOCKS - 1)
        exchange.pair(1).start()
        for copy in exchange.along_x(0):
            copy.start()

        @pl.loop(0, BLOCKS // 2)
        def _(step):
            scatter_block(
                step * 2 * BLOCK, 2 * BLOCK, vr_ref, hotc_ref, hic_ref, pr_ref, 4, right_place, 0, 1, 2
            )

            @pl.when(step == BLOCKS // 2 - 2)
            def _():
                exchange.after_pair(1)

        for copy in exchange.along_x(1):
            copy.start()
        exchange.after_y(0)
        exchange.after_x(0)
        exchange.after_y(1)
        exchange.after_x(1)
        exchange.end()

    pl.run_scoped(
        local,
        pltpu.VMEM((256, 1536), bf16),
        pltpu.VMEM(((LEFT_STEPS + RIGHT_STEPS) * 64, 256), bf16),
        pltpu.VMEM((1024, 256), bf16),
        pltpu.VMEM((256, 2 * SPT), bf16),
        pltpu.VMEM((256, 2 * SPT), bf16),
        pltpu.VMEM((32, 2 * SPT), bf16),
        pltpu.VMEM((64, 2 * SPT), bf16),
    )


def finish_kernel(la_ref, lb_ref, ra_ref, rb_ref, left_ref, right_ref):
    left_ref[...] = la_ref[...] + lb_ref[...]
    right_ref[...] = ra_ref[...] + rb_ref[...]


def on_device(coarse_left, coarse_right, sl, wl, sr, wr, mask, rows, cols, vals):
    vmem = pl.BlockSpec(memory_space=pltpu.VMEM)
    anywhere = pl.BlockSpec(memory_space=pl.ANY)
    operands = (
        mask.reshape(1, 2), coarse_left, coarse_right, sl.reshape(1, -1), wl, sr.reshape(1, -1), wr,
        rows, cols, vals,
    )
    dma = pltpu.SemaphoreType.DMA
    block = (128, 128)
    la, lb, ra, rb = pl.pallas_call(
        step_kernel,
        out_shape=(jax.ShapeDtypeStruct(block, f32),) * 4,
        in_specs=[anywhere] * 10,
        out_specs=(anywhere,) * 4,
        scratch_shapes=[
            pltpu.SMEM((1, 2), i32),
            *[pltpu.VMEM(a.shape, a.dtype) for a in operands[1:]],
            dma((10,)),
            dma((2,)),
            pltpu.VMEM((16, 2, 2304), f32),
            pltpu.VMEM((8, 4, 1280), f32),
            pltpu.VMEM((32, 512 * LEFT_STEPS), f32),
            pltpu.VMEM((32, 512 * RIGHT_STEPS), f32),
            pltpu.VMEM((8, 512 * LEFT_STEPS), f32),
            pltpu.VMEM((8, 512 * RIGHT_STEPS), f32),
            pltpu.VMEM((32, 2 * SPT), f32),
            pltpu.VMEM((32, 2 * SPT), f32),
            pltpu.VMEM((16, *block), f32),
            pltpu.VMEM((8, *block), f32),
            pltpu.VMEM((8, *block), f32),
            pltpu.VMEM((8, *block), f32),
            pltpu.VMEM((3, 2, *block), f32),
            pltpu.VMEM((2, *block), f32),
            pltpu.VMEM((2, 3, *block), f32),
            pltpu.VMEM((2, *block), f32),
            dma((4,)), dma((4,)), dma((23,)), dma((23,)), dma((23,)), dma((23,)),
            dma((17,)), dma((17,)),
        ],
        compiler_params=pltpu.CompilerParams(collective_id=0, has_side_effects=True),
        name="fused_step",
    )(*operands)
    left_sum, right_sum = pl.pallas_call(
        finish_kernel,
        out_shape=(jax.ShapeDtypeStruct(block, f32),) * 2,
        in_specs=[vmem] * 4,
        out_specs=(vmem,) * 2,
        name="finish",
    )(la, lb, ra, rb)
    left_new = left_sum.reshape(64, 2, 128).transpose(1, 0, 2).reshape(2, 8192)
    right_new = right_sum.reshape(32, 4, 128).transpose(1, 0, 2).reshape(4, 4096)
    return left_new, right_new


def solution(mesh):
    in_specs = (
        P("col", "row"),
        P("row", "col"),
        P("row"),
        P(None, "row"),
        P("col"),
        P(None, "col"),
        P("row", "col"),
        P("row", "col", None),
        P("row", "col", None),
        P("row", "col", None),
    )
    out_specs = (P("col", "row"), P("row", "col"))
    return jax.shard_map(
        on_device, mesh=mesh, in_specs=in_specs, out_specs=out_specs, check_vma=False
    )
```
